32 devices in a mesh: space: 2 (over core), energy: 8 (over z, y), mom: 2 (over x).
Axes of the slice: x: 2, y: 2, z: 4, core: 2. Of those that a mesh axis runs over, the one named last changes fastest.
Arguments:
- hamiltonian: float32 [2, 256, 256], P('space'), may hold values from -0.375 to 0.375
- coupling: float32 [2, 224, 224], P('space'), may hold values from -0.75 to 0.75
- self_energy: float32 [2, 8, 4, 2, 256, 256], P('space', 'energy', 'mom'), may hold values from -0.375 to 0.375
- pattern: int32 [2, 256, 256], P('space', 'energy'), may hold values 0 or 1
- momentum_table: int32 [4, 4], replicated, may hold values from 0 to 3
- momentum_weights: float32 [4], replicated, may hold values from 0.2 to 1
- mode_strengths: float32 [2], replicated, may hold values from 0.3 to 1
- mode_offsets: int32 [2], replicated, may hold values from 1 to 5
Outputs:
- new_self_energy: float32 [2, 8, 4, 2, 256, 256], P('space', 'energy', 'mom')
The draws below stay inside these ranges and needn't reach their ends.
Inputs may be any that keep to these rules, and one draw needn't show every extreme that they name: `momentum_table`: entry [k, q] is the momentum index whose Green's function reaches momentum k through transfer q.
All inputs are finite; a program needn't handle non-finite values. No bound on the sum of `pattern` on one device may be relied on, other than what follows from the above.
Results may differ from the reference program's by a relative error of at most 0.0001.
Values sent between devices are 32-bit elements; how exact they have to be, the bound alone decides.
No kernel may reach another device: no remote copies, remote signals or barrier semaphores. Data moves between devices by JAX's collectives and lax.ppermute only.
A program may use at most 128 MiB of HBM per device.

```python
import math
import jax
import jax.numpy as jnp
from jax import lax

ORB = 256
SURF = 224
MODES = 2
SLICES = 2
ENERGIES = 8
MOMENTA = 4


def with_ends(entries, own_key, least, high):
    index_at = [jax.random.randint(jax.random.fold_in(own_key, axis), (), 0, length) for axis, length in enumerate(entries.shape)]
    main_axis = entries.shape.index(max(entries.shape))
    neighbour = index_at[:main_axis] + [(index_at[main_axis] + 1) % entries.shape[main_axis]] + index_at[main_axis + 1:]
    return entries.at[tuple(index_at)].set(least).at[tuple(neighbour)].set(high)


def levels(stream_key, extent, split, smallest, high):
    gain = 1.0
    for position, shards_of in split:
        heights = jax.random.uniform(jax.random.fold_in(jax.random.fold_in(stream_key, 6), position), (shards_of,), jnp.float32, smallest / len(split), high / len(split))
        gain = gain * jnp.repeat(jnp.exp(heights), extent[position] // shards_of).reshape((-1,) + (1,) * (len(extent) - 1 - position))
    return gain


def centred(key, extent, scale, reach, split=(), kind=jnp.bfloat16):
    values = scale * jax.random.normal(key, extent, jnp.float32)
    if split:
        values = values * levels(key, extent, split, -0.22, 0.18)
    return jnp.clip(values, -reach, reach).astype(kind)


def setup_inputs(seed: int = 0) -> dict:
    key_list = jax.random.split(jax.random.key(seed), 9)
    hamiltonian = centred(key_list[0], (SLICES, ORB, ORB), ORB ** -0.5, 0.375, ((0, 2),), jnp.float32)
    coupling = centred(key_list[1], (SLICES, SURF, SURF), (SURF // 3) ** -0.5, 0.75, ((0, 2),), jnp.float32)
    self_energy = centred(key_list[2], (SLICES, ENERGIES, MOMENTA, 2, ORB, ORB), ORB ** -0.5, 0.375, ((0, 2), (1, 8), (2, 2)), jnp.float32)
    pattern = with_ends((jax.random.randint(key_list[3], (SLICES, ORB, ORB), 0, 4) < 3).astype(jnp.int32), jax.random.fold_in(key_list[3], 1), 0, 1)
    momentum_table = with_ends(jax.random.randint(key_list[4], (MOMENTA, MOMENTA), 0, MOMENTA), jax.random.fold_in(key_list[4], 1), 0, MOMENTA - 1).astype(jnp.int32)
    momentum_weights = jnp.clip(jnp.exp(jax.random.uniform(key_list[5], (MOMENTA,), jnp.float32, math.log(0.2), math.log(1.0))), 0.2, 1.0)
    mode_strengths = jnp.clip(jnp.exp(jax.random.uniform(key_list[6], (MODES,), jnp.float32, math.log(0.3), math.log(1.0))), 0.3, 1.0)
    mode_offsets = jax.random.randint(key_list[7], (MODES,), 1, ENERGIES * 3 // 4).astype(jnp.int32)
    return dict(hamiltonian=hamiltonian, coupling=coupling, self_energy=self_energy, pattern=pattern, momentum_table=momentum_table, momentum_weights=momentum_weights, mode_strengths=mode_strengths, mode_offsets=mode_offsets)


broadening = 1.0
contact = 1.0
dispersion = 1.0


def matmul_highest(left_side, right_side):
    return jnp.einsum('...ij,...jk->...ik', left_side, right_side, precision=lax.Precision.HIGHEST)


def product_complex(left_side, right_side):
    left_real = left_side[..., 0, :, :]
    left_imag = left_side[..., 1, :, :]
    right_real = right_side[..., 0, :, :]
    right_imag = right_side[..., 1, :, :]
    real_part = matmul_highest(left_real, right_real) - matmul_highest(left_imag, right_imag)
    imag_part = matmul_highest(left_real, right_imag) + matmul_highest(left_imag, right_real)
    return jnp.stack([real_part, imag_part], axis=-3)


def approximate_inverse(matrix):
    order_size = matrix.shape[-1]
    identity = jnp.eye(order_size, dtype=jnp.float32)
    real_part = matrix[..., 0, :, :]
    imag_part = matrix[..., 1, :, :]
    diag_real = jnp.diagonal(real_part, axis1=-2, axis2=-1)
    diag_imag = jnp.diagonal(imag_part, axis1=-2, axis2=-1)
    modulus = diag_real * diag_real + diag_imag * diag_imag
    inverse_real = diag_real / modulus
    inverse_imag = -diag_imag / modulus
    outside = 1.0 - identity
    off_real = real_part * outside
    off_imag = imag_part * outside
    row_real = inverse_real[..., :, None]
    row_imag = inverse_imag[..., :, None]
    scaled = jnp.stack([row_real * off_real - row_imag * off_imag, row_real * off_imag + row_imag * off_real], axis=-3)
    series = product_complex(scaled, scaled) - scaled
    series_real = series[..., 0, :, :] + identity
    series_imag = series[..., 1, :, :]
    column_real = inverse_real[..., None, :]
    column_imag = inverse_imag[..., None, :]
    return jnp.stack([series_real * column_real - series_imag * column_imag, series_real * column_imag + series_imag * column_real], axis=-3)


def build_system(hamiltonian_slice, self_slice, energy_index, momentum_index, energies_all, momenta_all):
    order_size = hamiltonian_slice.shape[-1]
    identity = jnp.eye(order_size, dtype=jnp.float32)
    symmetric = 0.5 * (hamiltonian_slice + hamiltonian_slice.T)
    energy = -2.0 + 4.0 * energy_index.astype(jnp.float32) / energies_all
    kinetic = dispersion * (1.0 - jnp.cos(2.0 * jnp.pi * momentum_index.astype(jnp.float32) / momenta_all))
    diagonal_shift = energy[:, None] - kinetic[None, :]
    real_part = diagonal_shift[:, :, None, None] * identity - symmetric - self_slice[:, :, 0]
    imag_part = broadening * identity - self_slice[:, :, 1]
    return jnp.stack([real_part, imag_part], axis=2)


def contact_term(surface):
    return jnp.stack([jnp.zeros((surface, surface), jnp.float32), -contact * jnp.eye(surface, dtype=jnp.float32)])


def embed_first(matrix, term):
    width = term.shape[-1]
    return matrix.at[..., :width, :width].add(-term)


def embed_last(matrix, term):
    width = term.shape[-1]
    order_size = matrix.shape[-1]
    return matrix.at[..., order_size - width:, order_size - width:].add(-term)


def sandwich(coupling_block, middle):
    return jnp.einsum('ji,...jk,kl->...il', coupling_block, middle, coupling_block, precision=lax.Precision.HIGHEST)


def sandwich_back(coupling_block, middle):
    return jnp.einsum('ij,...jk,lk->...il', coupling_block, middle, coupling_block, precision=lax.Precision.HIGHEST)


def convolve_energy(green_rows, mode_strengths, mode_offsets):
    point_count = green_rows.shape[0]
    widths = [(point_count, point_count)] + [(0, 0)] * (green_rows.ndim - 1)
    padded = jnp.pad(green_rows, widths)
    accumulated = jnp.zeros_like(green_rows)
    for mode_index in range(mode_strengths.shape[0]):
        offset_now = mode_offsets[mode_index].astype(jnp.int32)
        below_part = lax.dynamic_slice_in_dim(padded, (point_count - offset_now).astype(jnp.int32), point_count, 0)
        above_part = lax.dynamic_slice_in_dim(padded, (point_count + offset_now).astype(jnp.int32), point_count, 0)
        accumulated = accumulated + mode_strengths[mode_index] * (below_part + above_part)
    return accumulated


def momentum_coefficients(momentum_table, momentum_weights):
    momentum_count = momentum_table.shape[0]
    labels = jnp.arange(momentum_count, dtype=jnp.int32)
    matches = (momentum_table[:, :, None] == labels[None, None, :]).astype(jnp.float32)
    return jnp.einsum('q,kqj->kj', momentum_weights, matches, precision=lax.Precision.HIGHEST)


def reference(hamiltonian, coupling, self_energy, pattern, momentum_table, momentum_weights, mode_strengths, mode_offsets):
    slices = hamiltonian.shape[0]
    energy_index = jnp.arange(ENERGIES, dtype=jnp.int32)
    momentum_index = jnp.arange(MOMENTA, dtype=jnp.int32)
    item_shape = (ENERGIES, MOMENTA, 2, SURF, SURF)
    source = jnp.broadcast_to(contact_term(SURF), item_shape)

    def system_of(slice_index):
        return build_system(hamiltonian[slice_index], self_energy[slice_index], energy_index, momentum_index, ENERGIES, MOMENTA)

    left_terms = []
    incoming = source
    for slice_index in range(slices):
        left_terms.append(incoming)
        green_left = approximate_inverse(embed_first(system_of(slice_index), incoming))
        incoming = sandwich(coupling[slice_index], green_left[..., ORB - SURF:, ORB - SURF:])
    right_terms = [None] * slices
    incoming = source
    for slice_index in reversed(range(slices)):
        right_now = sandwich_back(coupling[slice_index], incoming)
        right_terms[slice_index] = right_now
        green_right = approximate_inverse(embed_last(system_of(slice_index), right_now))
        incoming = green_right[..., :SURF, :SURF]
    coefficients = momentum_coefficients(momentum_table, momentum_weights)
    outputs = []
    for slice_index in range(slices):
        green_final = approximate_inverse(embed_last(embed_first(system_of(slice_index), left_terms[slice_index]), right_terms[slice_index]))
        phonon = convolve_energy(green_final, mode_strengths, mode_offsets)
        mixed_terms = jnp.einsum('kj,ej...->ek...', coefficients, phonon, precision=lax.Precision.HIGHEST)
        outputs.append(mixed_terms * pattern[slice_index].astype(jnp.float32))
    return jnp.stack(outputs)
```

```python
import functools

import jax
import jax.numpy as jnp
from jax import lax
from jax.experimental import pallas as pl
from jax.experimental.pallas import tpu as pltpu
from jax.sharding import PartitionSpec as P

broadening = 1.0
contact = 1.0
dispersion = 1.0
parts = 2
kernel_memory = 24 * 1024 * 1024


def split_pair(value):
    high = value.astype(jnp.bfloat16)
    return high, (value - high.astype(jnp.float32)).astype(jnp.bfloat16)


def product(left_pair, right_pair):
    left_high, left_low = left_pair
    right_high, right_low = right_pair
    dot = functools.partial(jnp.dot, preferred_element_type=jnp.float32)
    return dot(left_high, right_high) + dot(left_high, right_low) + dot(left_low, right_high)


def diagonal_mask(order_size):
    rows = lax.broadcasted_iota(jnp.int32, (order_size, order_size), 0)
    columns = lax.broadcasted_iota(jnp.int32, (order_size, order_size), 1)
    return rows == columns


def inverse_pair(real_part, imag_part):
    order_size = real_part.shape[-1]
    on_diagonal = diagonal_mask(order_size)
    only_real = jnp.where(on_diagonal, real_part, 0.0)
    only_imag = jnp.where(on_diagonal, imag_part, 0.0)

    def reciprocal(axis):
        diag_real = jnp.sum(only_real, axis=axis, keepdims=True)
        diag_imag = jnp.sum(only_imag, axis=axis, keepdims=True)
        modulus = diag_real * diag_real + diag_imag * diag_imag
        return diag_real / modulus, -diag_imag / modulus

    row_real, row_imag = reciprocal(1)
    column_real, column_imag = reciprocal(0)
    off_real = jnp.where(on_diagonal, 0.0, real_part)
    off_imag = jnp.where(on_diagonal, 0.0, imag_part)
    scaled_real = row_real * off_real - row_imag * off_imag
    scaled_imag = row_real * off_imag + row_imag * off_real
    pair_real = split_pair(scaled_real)
    pair_imag = split_pair(scaled_imag)
    pair_both = split_pair(scaled_real + scaled_imag)
    square_real = product(pair_real, pair_real)
    square_imag = product(pair_imag, pair_imag)
    square_both = product(pair_both, pair_both)
    series_real = square_real - square_imag - scaled_real + jnp.where(on_diagonal, 1.0, 0.0)
    series_imag = square_both - square_real - square_imag - scaled_imag
    return (
        series_real * column_real - series_imag * column_imag,
        series_real * column_imag + series_imag * column_real,
    )


def start_kernel(
    surface, slice_ref, shift_ref, hamiltonian_ref, coupling_ref, self_ref, known_ref, face_ref,
    base_ref, term_ref, wide_ref, green_ref,
):
    order_size = hamiltonian_ref.shape[-1]
    corner = order_size - surface
    item = pl.program_id(0)
    slice_now = slice_ref[0]

    @pl.when(item == 0)
    def _():
        base_ref[...] = 0.5 * (hamiltonian_ref[0] + hamiltonian_ref[0].T)

        @pl.when(slice_now == 0)
        def _():
            rows = lax.broadcasted_iota(jnp.int32, (order_size, order_size), 0)
            inside = jnp.logical_and(diagonal_mask(order_size), rows < surface)
            term_ref[...] = jnp.where(inside, contact, 0.0)

        @pl.when(slice_now != 0)
        def _():
            wide_ref[...] = jnp.zeros_like(wide_ref)
            wide_ref[corner:, :surface] = coupling_ref[0]
            wide = wide_ref[...]
            term_ref[...] = contact * product(split_pair(wide), split_pair(wide.T))

    on_diagonal = diagonal_mask(order_size)
    real_part = jnp.where(on_diagonal, shift_ref[item], 0.0) - base_ref[...] - self_ref[0, 0]
    imag_part = jnp.where(on_diagonal, broadening, 0.0) - self_ref[0, 1] + term_ref[...]
    known_ref[0, 0] = real_part
    known_ref[0, 1] = imag_part
    green_real, green_imag = inverse_pair(real_part, imag_part)
    green_ref[0] = green_real
    green_ref[1] = green_imag
    first = pl.multiple_of(jnp.where(slice_now == 0, corner, 0), 8)
    face_ref[0] = green_ref[:, pl.ds(first, surface), :]


def finish_kernel(
    surface, pieces, slice_ref, coupling_ref, known_ref, face_ref, out_ref,
    wide_ref, side_high_ref, side_low_ref, across_high_ref, across_low_ref, face_full_ref,
):
    order_size = known_ref.shape[-1]
    corner = order_size - surface
    item = pl.program_id(0)
    slice_now = slice_ref[0]

    @pl.when(item == 0)
    def _():
        face_full_ref[...] = jnp.zeros_like(face_full_ref)
        wide_ref[...] = jnp.zeros_like(wide_ref)
        wide_ref[corner:, :surface] = coupling_ref[...]
        plain = wide_ref[...]
        turned = plain.T
        at_first = slice_now == 0
        side_high_ref[...], side_low_ref[...] = split_pair(jnp.where(at_first, plain, turned))
        across_high_ref[...], across_low_ref[...] = split_pair(jnp.where(at_first, turned, plain))

    first = pl.multiple_of(jnp.where(slice_now == 0, 0, corner), 8)
    face_full_ref[:, pl.ds(first, surface), :] = face_ref[0]
    side = (side_high_ref[...], side_low_ref[...])
    across = (across_high_ref[...], across_low_ref[...])
    through_real = product(side, split_pair(face_full_ref[0]))
    through_imag = product(side, split_pair(face_full_ref[1]))
    real_part = known_ref[0, 0] - product(split_pair(through_real), across)
    imag_part = known_ref[0, 1] - product(split_pair(through_imag), across)
    green = inverse_pair(real_part, imag_part)
    for piece, segments in enumerate(pieces):
        filled = 0
        for part, row, count in segments:
            out_ref[piece, 0, filled : filled + count, :] = green[part][row : row + count, :]
            filled += count


def scatter_kernel(
    energies_all, momenta_all, energies_here, momenta_here, momentum_groups, branches,
    offset_ref, strength_ref, coefficient_ref, mask_ref, in_ref, out_ref, mixed_ref,
):
    def place(energy, momentum):
        group = (energy // energies_here) * momentum_groups + momentum // momenta_here
        return group, (energy % energies_here) * momenta_here + momentum % momenta_here

    mixed_ref[energies_all] = jnp.zeros(mixed_ref.shape[1:], jnp.float32)
    for energy in range(energies_all):
        blocks = [in_ref[place(energy, momentum)] for momentum in range(momenta_all)]
        for target in range(momenta_all):
            total = coefficient_ref[target, 0] * blocks[0]
            for momentum in range(1, momenta_all):
                total = total + coefficient_ref[target, momentum] * blocks[momentum]
            mixed_ref[energy, target] = total
    mask = mask_ref[...].astype(jnp.float32)
    for energy in range(energies_all):
        sources = []
        for branch in range(branches):
            below = energy - offset_ref[branch]
            above = energy + offset_ref[branch]
            below = jnp.where(jnp.logical_and(below >= 0, below < energies_all), below, energies_all)
            above = jnp.where(jnp.logical_and(above >= 0, above < energies_all), above, energies_all)
            sources.append((strength_ref[branch], below, above))
        for target in range(momenta_all):
            total = None
            for strength, below, above in sources:
                term = strength * (mixed_ref[below, target] + mixed_ref[above, target])
                total = term if total is None else total + term
            out_ref[place(energy, target)] = total * mask


def row_pieces(order_size, energy_groups, momentum_groups):
    per_energy = order_size // energy_groups
    piece_rows = parts * per_energy // momentum_groups
    pieces = []
    for energy_group in range(energy_groups):
        for momentum_group in range(momentum_groups):
            start, left, segments = momentum_group * piece_rows, piece_rows, []
            while left:
                part, inside = divmod(start, per_energy)
                count = min(left, per_energy - inside)
                segments.append((part, energy_group * per_energy + inside, count))
                start, left = start + count, left - count
            pieces.append(segments)
    return per_energy, piece_rows, pieces


def momentum_coefficients(momentum_table, momentum_weights):
    momentum_count = momentum_table.shape[0]
    labels = jnp.arange(momentum_count, dtype=jnp.int32)
    matches = momentum_table[:, :, None] == labels[None, None, :]
    return jnp.sum(jnp.where(matches, momentum_weights[None, :, None], 0.0), axis=1)


def product_split(left_side, right_side):
    return product(split_pair(left_side), split_pair(right_side))


def green_by_sweeps(hamiltonian, coupling, self_blocks, shift, position, slices):
    orbitals, surface = hamiltonian.shape[-1], coupling.shape[-1]
    corner = orbitals - surface
    identity = jnp.eye(orbitals, dtype=jnp.float32)
    symmetric = 0.5 * (hamiltonian + hamiltonian.T)
    system = jnp.stack(
        [
            shift[:, None, None] * identity - symmetric - self_blocks[:, 0],
            broadening * identity - self_blocks[:, 1],
        ],
        axis=1,
    )
    source = jnp.stack([jnp.zeros((surface, surface)), -contact * jnp.eye(surface)]).astype(jnp.float32)
    source = jnp.broadcast_to(source, (system.shape[0],) + source.shape)
    over_parts = jax.vmap(jax.vmap(product_split, (None, 0)), (None, 0))
    over_parts_right = jax.vmap(jax.vmap(product_split, (0, None)), (0, None))
    around = ((0, 0), (0, 0))

    def less_first(matrix, term):
        return matrix - jnp.pad(term, around + ((0, corner), (0, corner)))

    def less_last(matrix, term):
        return matrix - jnp.pad(term, around + ((corner, 0), (corner, 0)))

    def inverse(matrix):
        return jnp.stack(jax.vmap(inverse_pair)(matrix[:, 0], matrix[:, 1]), axis=1)

    def through(side, middle):
        return over_parts_right(over_parts(side, middle), side.T)

    left = source
    right = through(coupling, source)
    for turn in range(slices - 1):
        face = inverse(less_first(system, left))[..., corner:, corner:]
        moved = lax.ppermute(through(coupling.T, face), "space", [(i, i + 1) for i in range(slices - 1)])
        left = jnp.where(position == turn + 1, moved, left)
        face = inverse(less_last(system, right))[..., :surface, :surface]
        moved = lax.ppermute(face, "space", [(i + 1, i) for i in range(slices - 1)])
        right = jnp.where(position == slices - 2 - turn, through(coupling, moved), right)
    return inverse(less_last(less_first(system, left), right))


def cut_pieces(green, pieces):
    return jnp.stack(
        [
            jnp.concatenate([green[:, part, row : row + count] for part, row, count in segments], axis=1)
            for segments in pieces
        ]
    )


def on_chip(*block):
    return pl.BlockSpec(memory_space=pltpu.SMEM)


def resident(shape):
    return pl.BlockSpec(shape, lambda item: (0,) * len(shape))


def per_item(shape):
    return pl.BlockSpec((1,) + shape, lambda item: (item,) + (0,) * len(shape))


float_vmem = functools.partial(pltpu.VMEM, dtype=jnp.float32)
half_vmem = functools.partial(pltpu.VMEM, dtype=jnp.bfloat16)


def green_two_slices(hamiltonian, coupling, self_blocks, shift, position, pieces, blocks_shape):
    orbitals, surface = hamiltonian.shape[-1], coupling.shape[-1]
    items = self_blocks.shape[0]
    slice_now = position.astype(jnp.int32).reshape(1)
    order = (orbitals, orbitals)

    swap = [(0, 1), (1, 0)]
    first_coupling = lax.ppermute(coupling[0], "space", swap)
    first_coupling = jnp.where(position == 0, coupling[0], first_coupling)
    known, face = pl.pallas_call(
        functools.partial(start_kernel, surface),
        grid=(items,),
        in_specs=[
            on_chip(), on_chip(), resident((1,) + order), resident((1, surface, surface)), per_item((parts,) + order),
        ],
        out_specs=[per_item((parts,) + order), per_item((parts, surface, orbitals))],
        out_shape=[
            jax.ShapeDtypeStruct((items, parts) + order, jnp.float32),
            jax.ShapeDtypeStruct((items, parts, surface, orbitals), jnp.float32),
        ],
        scratch_shapes=[float_vmem(order), float_vmem(order), float_vmem(order), float_vmem((parts,) + order)],
        compiler_params=pltpu.CompilerParams(vmem_limit_bytes=kernel_memory),
        name="start",
    )(slice_now, shift, hamiltonian, coupling, self_blocks)
    face = lax.ppermute(face, "space", swap)

    return pl.pallas_call(
        functools.partial(finish_kernel, surface, pieces),
        grid=(items,),
        in_specs=[
            on_chip(), resident((surface, surface)), per_item((parts,) + order), per_item((parts, surface, orbitals)),
        ],
        out_specs=pl.BlockSpec((blocks_shape[0], 1) + blocks_shape[2:], lambda item: (0, item, 0, 0)),
        out_shape=jax.ShapeDtypeStruct(blocks_shape, jnp.float32),
        scratch_shapes=[float_vmem(order)] + [half_vmem(order)] * 4 + [float_vmem((parts,) + order)],
        compiler_params=pltpu.CompilerParams(vmem_limit_bytes=kernel_memory),
        name="finish",
    )(slice_now, first_coupling, known, face)


def body(
    hamiltonian,
    coupling,
    self_energy,
    pattern,
    momentum_table,
    momentum_weights,
    mode_strengths,
    mode_offsets,
):
    orbitals = hamiltonian.shape[-1]
    surface = coupling.shape[-1]
    energies_here = self_energy.shape[1]
    momenta_here = self_energy.shape[2]
    energy_groups = lax.axis_size("energy")
    momentum_groups = lax.axis_size("mom")
    position = lax.axis_index("space")
    energies_all = energies_here * energy_groups
    momenta_all = momenta_here * momentum_groups
    items = energies_here * momenta_here
    branches = mode_offsets.shape[0]
    energy_index = lax.axis_index("energy") * energies_here + jnp.arange(energies_here, dtype=jnp.int32)
    momentum_index = lax.axis_index("mom") * momenta_here + jnp.arange(momenta_here, dtype=jnp.int32)
    energy = -2.0 + 4.0 * energy_index.astype(jnp.float32) / energies_all
    angle = 2.0 * jnp.pi * momentum_index.astype(jnp.float32) / momenta_all
    kinetic = dispersion * (1.0 - jnp.cos(angle))
    shift = (energy[:, None] - kinetic[None, :]).reshape(items)
    self_blocks = self_energy.reshape(items, parts, orbitals, orbitals)
    per_energy, piece_rows, pieces = row_pieces(orbitals, energy_groups, momentum_groups)
    blocks_shape = (len(pieces), items, piece_rows, orbitals)
    if lax.axis_size("space") == 2:
        green = green_two_slices(hamiltonian, coupling, self_blocks, shift, position, pieces, blocks_shape)
    else:
        slices = lax.axis_size("space")
        green = green_by_sweeps(hamiltonian[0], coupling[0], self_blocks, shift, position, slices)
        green = cut_pieces(green, pieces)

    everyone = ("energy", "mom")
    gathered = lax.all_to_all(green, everyone, split_axis=0, concat_axis=0, tiled=True)
    coefficients = momentum_coefficients(momentum_table, momentum_weights)
    mask_rows = jnp.concatenate([pattern[0]] * parts, axis=0)
    mask_rows = lax.dynamic_slice_in_dim(mask_rows, lax.axis_index("mom") * piece_rows, piece_rows, 0)
    scattered = pl.pallas_call(
        functools.partial(
            scatter_kernel, energies_all, momenta_all, energies_here, momenta_here, momentum_groups, branches
        ),
        in_specs=[on_chip(), on_chip(), on_chip(), pl.BlockSpec(), pl.BlockSpec()],
        out_shape=jax.ShapeDtypeStruct(blocks_shape, jnp.float32),
        scratch_shapes=[float_vmem((energies_all + 1, momenta_all, piece_rows, orbitals))],
        compiler_params=pltpu.CompilerParams(vmem_limit_bytes=kernel_memory),
        name="scatter",
    )(mode_offsets, mode_strengths, coefficients, mask_rows, gathered)
    returned = lax.all_to_all(scattered, everyone, split_axis=0, concat_axis=0, tiled=True)
    returned = returned.reshape(energy_groups, momentum_groups, items, piece_rows, orbitals)
    returned = returned.transpose(2, 0, 1, 3, 4).reshape(items, energy_groups, parts, per_energy, orbitals)
    returned = returned.transpose(0, 2, 1, 3, 4)
    return returned.reshape(1, energies_here, momenta_here, parts, orbitals, orbitals)


def solution(mesh):
    return jax.shard_map(
        body,
        mesh=mesh,
        in_specs=(
            P("space", None, None),
            P("space", None, None),
            P("space", "energy", "mom", None, None, None),
            P("space", "energy", None),
            P(),
            P(),
            P(),
            P(),
        ),
        out_specs=P("space", "energy", "mom", None, None, None),
        check_vma=False,
    )
```

```python
import functools

import jax
import jax.numpy as jnp
from jax import lax
from jax.experimental import pallas as pl
from jax.experimental.pallas import tpu as pltpu
from jax.sharding import PartitionSpec as P

broadening = 1.0
contact = 1.0
dispersion = 1.0
parts = 2
kernel_memory = 24 * 1024 * 1024


def split_pair(value):
    high = value.astype(jnp.bfloat16)
    return high, (value - high.astype(jnp.float32)).astype(jnp.bfloat16)


def product(left_pair, right_pair):
    left_high, left_low = left_pair
    right_high, right_low = right_pair
    dot = functools.partial(jnp.dot, preferred_element_type=jnp.float32)
    return dot(left_high, right_high) + dot(left_high, right_low) + dot(left_low, right_high)


def diagonal_mask(order_size):
    rows = lax.broadcasted_iota(jnp.int32, (order_size, order_size), 0)
    columns = lax.broadcasted_iota(jnp.int32, (order_size, order_size), 1)
    return rows == columns


def product_stacked(left_pairs, right_pair):
    rows = left_pairs[0][0].shape[0]
    count = len(left_pairs)
    right_high, right_low = right_pair
    highs = [pair[0] for pair in left_pairs]
    lows = [pair[1] for pair in left_pairs]
    dot = functools.partial(jnp.dot, preferred_element_type=jnp.float32)
    with_high = dot(jnp.concatenate(highs + lows, axis=0), right_high)
    with_low = dot(jnp.concatenate(highs, axis=0), right_low)
    return [
        with_high[i * rows : (i + 1) * rows]
        + with_high[(count + i) * rows : (count + i + 1) * rows]
        + with_low[i * rows : (i + 1) * rows]
        for i in range(count)
    ]


def inverse_pair(real_part, imag_part):
    order_size = real_part.shape[-1]
    on_diagonal = diagonal_mask(order_size)
    diag_real = jnp.sum(jnp.where(on_diagonal, real_part, 0.0), axis=0, keepdims=True)
    diag_imag = jnp.sum(jnp.where(on_diagonal, imag_part, 0.0), axis=0, keepdims=True)
    modulus = diag_real * diag_real + diag_imag * diag_imag
    column_real = diag_real / modulus
    column_imag = -diag_imag / modulus
    row_real = jnp.sum(jnp.where(on_diagonal, column_real, 0.0), axis=1, keepdims=True)
    row_imag = jnp.sum(jnp.where(on_diagonal, column_imag, 0.0), axis=1, keepdims=True)
    off_real = jnp.where(on_diagonal, 0.0, real_part)
    off_imag = jnp.where(on_diagonal, 0.0, imag_part)
    scaled_real = row_real * off_real - row_imag * off_imag
    scaled_imag = row_real * off_imag + row_imag * off_real
    pair_real = split_pair(scaled_real)
    pair_imag = split_pair(scaled_imag)
    pair_both = split_pair(scaled_real + scaled_imag)
    (square_real,) = product_stacked([pair_real], pair_real)
    (square_imag,) = product_stacked([pair_imag], pair_imag)
    (square_both,) = product_stacked([pair_both], pair_both)
    series_real = square_real - square_imag - scaled_real + jnp.where(on_diagonal, 1.0, 0.0)
    series_imag = square_both - square_real - square_imag - scaled_imag
    return (
        series_real * column_real - series_imag * column_imag,
        series_real * column_imag + series_imag * column_real,
    )


def start_kernel(item, items, surface, slice_ref, shift_ref, base_from_ref, term_from_ref, *rest):
    slice_now = slice_ref[0]
    if item == 0:
        self_from_ref, known_ref, face_ref, base_ref, term_ref = rest[:5]
        later_refs = rest[5 : 4 + items]
        self_ref, green_ref, base_buffer, coupling_buffer, wide_ref, semaphores = rest[4 + items :]
        self_copies = []
        for place, target_ref in enumerate((self_ref,) + later_refs):
            for part in range(parts):
                semaphore = semaphores.at[2 + place * parts + part]
                copy = pltpu.make_async_copy(self_from_ref.at[place, part], target_ref.at[part], semaphore)
                self_copies.append(copy)
        coupling_copy = pltpu.make_async_copy(term_from_ref.at[0], coupling_buffer, semaphores.at[0])
        base_copy = pltpu.make_async_copy(base_from_ref.at[0], base_buffer, semaphores.at[1])
        for copy in [coupling_copy, base_copy] + self_copies:
            copy.start()
    else:
        self_ref, known_ref, face_ref, green_ref = rest
        base_ref, term_ref = base_from_ref, term_from_ref
    order_size = known_ref.shape[-1]
    corner = order_size - surface
    on_diagonal = diagonal_mask(order_size)
    if item == 0:
        coupling_copy.wait()
        face_ref[parts] = jnp.zeros(face_ref.shape[1:], jnp.float32)
        face_ref[parts, :, :surface] = coupling_buffer[...]

        @pl.when(slice_now == 0)
        def _():
            rows = lax.broadcasted_iota(jnp.int32, (order_size, order_size), 0)
            inside = jnp.logical_and(on_diagonal, rows < surface)
            term_ref[...] = jnp.where(inside, contact, 0.0)

        @pl.when(slice_now != 0)
        def _():
            wide_ref[...] = jnp.zeros_like(wide_ref)
            wide_ref[corner:, :surface] = coupling_buffer[...]
            wide = wide_ref[...]
            term_ref[...] = contact * product(split_pair(wide), split_pair(wide.T))

        base_copy.wait()
        base_ref[...] = 0.5 * (base_buffer[...] + base_buffer[...].T)
        for copy in self_copies[:parts]:
            copy.wait()
    real_part = jnp.where(on_diagonal, shift_ref[item], 0.0) - base_ref[...] - self_ref[0]
    imag_part = jnp.where(on_diagonal, broadening, 0.0) - self_ref[1] + term_ref[...]
    known_ref[0] = real_part
    known_ref[1] = imag_part
    green_real, green_imag = inverse_pair(real_part, imag_part)
    green_ref[0] = green_real
    green_ref[1] = green_imag
    first = pl.multiple_of(jnp.where(slice_now == 0, corner, 0), 8)
    face_ref[:parts] = green_ref[:, pl.ds(first, surface), :]
    if item == 0:
        for copy in self_copies[parts:]:
            copy.wait()


def finish_kernel(item, items, surface, pieces, *refs):
    last = item == items - 1
    slice_ref, known_ref, face_ref = refs[:3]
    refs = refs[3:]
    if item == 0:
        own_ref, refs = refs[0], refs[1:]
    else:
        sides, refs = refs[:4], refs[4:]
    earlier_refs, refs = (refs[:item], refs[item:]) if last else ((), refs)
    out_ref, refs = refs[0], refs[1:]
    if item == 0:
        sides, refs = refs[:4], refs[4:]
    side_high_ref, side_low_ref, across_high_ref, across_low_ref = sides
    face_full_ref = refs[0]
    if item == 0:
        wide_ref = refs[1]
    order_size = known_ref.shape[-1]
    corner = order_size - surface
    slice_now = slice_ref[0]
    face_full_ref[...] = jnp.zeros_like(face_full_ref)
    if item == 0:
        wide_ref[...] = jnp.zeros_like(wide_ref)

        @pl.when(slice_now == 0)
        def _():
            wide_ref[corner:, :surface] = own_ref[parts, :, :surface]
            plain = wide_ref[...]
            side_high_ref[...], side_low_ref[...] = split_pair(plain)
            across_high_ref[...], across_low_ref[...] = split_pair(plain.T)

        @pl.when(slice_now != 0)
        def _():
            wide_ref[corner:, :surface] = face_ref[parts, :, :surface]
            plain = wide_ref[...]
            side_high_ref[...], side_low_ref[...] = split_pair(plain.T)
            across_high_ref[...], across_low_ref[...] = split_pair(plain)

    first = pl.multiple_of(jnp.where(slice_now == 0, 0, corner), 8)
    face_full_ref[:, pl.ds(first, surface), :] = face_ref[:parts]
    side = (side_high_ref[...], side_low_ref[...])
    across = (across_high_ref[...], across_low_ref[...])
    (through_real,) = product_stacked([side], split_pair(face_full_ref[0]))
    (through_imag,) = product_stacked([side], split_pair(face_full_ref[1]))
    term_real, term_imag = product_stacked([split_pair(through_real), split_pair(through_imag)], across)
    green = inverse_pair(known_ref[0] - term_real, known_ref[1] - term_imag)
    for piece, segments in enumerate(pieces):
        filled = 0
        for part, row, count in segments:
            target = (piece, item) if last else (piece,)
            out_ref[target + (slice(filled, filled + count), slice(None))] = green[part][row : row + count, :]
            filled += count
    for place, earlier_ref in enumerate(earlier_refs):
        out_ref[:, place] = earlier_ref[...]


def scatter_kernel(
    energies_all, momenta_all, energies_here, momenta_here, momentum_groups, branches,
    offset_ref, strength_ref, coefficient_ref, mask_ref, in_ref, out_ref, mixed_ref,
):
    def place(energy, momentum):
        group = (energy // energies_here) * momentum_groups + momentum // momenta_here
        return group, (energy % energies_here) * momenta_here + momentum % momenta_here

    mixed_ref[energies_all] = jnp.zeros(mixed_ref.shape[1:], jnp.float32)
    for energy in range(energies_all):
        blocks = [in_ref[place(energy, momentum)] for momentum in range(momenta_all)]
        for target in range(momenta_all):
            total = coefficient_ref[target, 0] * blocks[0]
            for momentum in range(1, momenta_all):
                total = total + coefficient_ref[target, momentum] * blocks[momentum]
            mixed_ref[energy, target] = total
    mask = mask_ref[...].astype(jnp.float32)
    for energy in range(energies_all):
        sources = []
        for branch in range(branches):
            below = energy - offset_ref[branch]
            above = energy + offset_ref[branch]
            below = jnp.where(jnp.logical_and(below >= 0, below < energies_all), below, energies_all)
            above = jnp.where(jnp.logical_and(above >= 0, above < energies_all), above, energies_all)
            sources.append((strength_ref[branch], below, above))
        for target in range(momenta_all):
            total = None
            for strength, below, above in sources:
                term = strength * (mixed_ref[below, target] + mixed_ref[above, target])
                total = term if total is None else total + term
            out_ref[place(energy, target)] = total * mask


def row_pieces(order_size, energy_groups, momentum_groups):
    per_energy = order_size // energy_groups
    piece_rows = parts * per_energy // momentum_groups
    pieces = []
    for energy_group in range(energy_groups):
        for momentum_group in range(momentum_groups):
            start, left, segments = momentum_group * piece_rows, piece_rows, []
            while left:
                part, inside = divmod(start, per_energy)
                count = min(left, per_energy - inside)
                segments.append((part, energy_group * per_energy + inside, count))
                start, left = start + count, left - count
            pieces.append(segments)
    return per_energy, piece_rows, pieces


def momentum_coefficients(momentum_table, momentum_weights):
    momentum_count = momentum_table.shape[0]
    labels = jnp.arange(momentum_count, dtype=jnp.int32)
    matches = momentum_table[:, :, None] == labels[None, None, :]
    return jnp.sum(jnp.where(matches, momentum_weights[None, :, None], 0.0), axis=1)


def product_split(left_side, right_side):
    return product(split_pair(left_side), split_pair(right_side))


def green_by_sweeps(hamiltonian, coupling, self_blocks, shift, position, slices):
    orbitals, surface = hamiltonian.shape[-1], coupling.shape[-1]
    corner = orbitals - surface
    identity = jnp.eye(orbitals, dtype=jnp.float32)
    symmetric = 0.5 * (hamiltonian + hamiltonian.T)
    system = jnp.stack(
        [
            shift[:, None, None] * identity - symmetric - self_blocks[:, 0],
            broadening * identity - self_blocks[:, 1],
        ],
        axis=1,
    )
    source = jnp.stack([jnp.zeros((surface, surface)), -contact * jnp.eye(surface)]).astype(jnp.float32)
    source = jnp.broadcast_to(source, (system.shape[0],) + source.shape)
    over_parts = jax.vmap(jax.vmap(product_split, (None, 0)), (None, 0))
    over_parts_right = jax.vmap(jax.vmap(product_split, (0, None)), (0, None))
    around = ((0, 0), (0, 0))

    def less_first(matrix, term):
        return matrix - jnp.pad(term, around + ((0, corner), (0, corner)))

    def less_last(matrix, term):
        return matrix - jnp.pad(term, around + ((corner, 0), (corner, 0)))

    def inverse(matrix):
        return jnp.stack(jax.vmap(inverse_pair)(matrix[:, 0], matrix[:, 1]), axis=1)

    def through(side, middle):
        return over_parts_right(over_parts(side, middle), side.T)

    left = source
    right = through(coupling, source)
    for turn in range(slices - 1):
        face = inverse(less_first(system, left))[..., corner:, corner:]
        moved = lax.ppermute(through(coupling.T, face), "space", [(i, i + 1) for i in range(slices - 1)])
        left = jnp.where(position == turn + 1, moved, left)
        face = inverse(less_last(system, right))[..., :surface, :surface]
        moved = lax.ppermute(face, "space", [(i + 1, i) for i in range(slices - 1)])
        right = jnp.where(position == slices - 2 - turn, through(coupling, moved), right)
    return inverse(less_last(less_first(system, left), right))


def cut_pieces(green, pieces):
    return jnp.stack(
        [
            jnp.concatenate([green[:, part, row : row + count] for part, row, count in segments], axis=1)
            for segments in pieces
        ]
    )


def on_chip(*block):
    return pl.BlockSpec(memory_space=pltpu.SMEM)


float_vmem = functools.partial(pltpu.VMEM, dtype=jnp.float32)


def green_two_slices(hamiltonian, coupling, self_blocks, shift, position, pieces, blocks_shape):
    orbitals, surface = hamiltonian.shape[-1], coupling.shape[-1]
    items = self_blocks.shape[0]
    slice_now = position.astype(jnp.int32).reshape(1)
    order = (orbitals, orbitals)
    pair = (parts,) + order
    floats = functools.partial(jax.ShapeDtypeStruct, dtype=jnp.float32)
    halves = functools.partial(jax.ShapeDtypeStruct, dtype=jnp.bfloat16)
    whole = pl.BlockSpec(memory_space=pltpu.VMEM)
    far = pl.BlockSpec(memory_space=pltpu.HBM)
    params = pltpu.CompilerParams(vmem_limit_bytes=kernel_memory)
    inverse_flops = 18 * orbitals**3
    swap = [(0, 1), (1, 0)]

    self_blocks, base, term = (
        pltpu.with_memory_space_constraint(array, pltpu.HBM) for array in (self_blocks, hamiltonian, coupling)
    )
    known, faces, sent = [], [], []
    later = []
    for item in range(items):
        first = item == 0
        scratch = [float_vmem(pair)]
        if first:
            scratch += [float_vmem(pair), float_vmem(order), float_vmem((surface, surface)), float_vmem(order)]
            scratch += [pltpu.SemaphoreType.DMA((2 + items * parts,))]
        extra_shapes = [floats(order), floats(order)] + [floats(pair)] * (items - 1) if first else []
        result = pl.pallas_call(
            functools.partial(start_kernel, item, items, surface),
            in_specs=[on_chip(), on_chip()] + [far if first else whole] * 3,
            out_specs=[whole] * (2 + len(extra_shapes)),
            out_shape=[floats(pair), floats((parts + first, surface, orbitals))] + extra_shapes,
            scratch_shapes=scratch,
            compiler_params=params,
            cost_estimate=pl.CostEstimate(flops=inverse_flops, bytes_accessed=0, transcendentals=0),
            name=f"start{item}",
        )(slice_now, shift, base, term, self_blocks if first else later[item - 1])
        known.append(result[0])
        if first:
            base, term, *later = result[2:]
        sent.append(result[1])
        faces.append(lax.ppermute(result[1], "space", swap))

    greens, sides = [], []
    for item in range(items):
        first, last = item == 0, item == items - 1
        operands = [slice_now, known[item], faces[item]] + ([sent[item]] if first else sides) + (greens if last else [])
        out_shape = [floats(blocks_shape if last else blocks_shape[:1] + blocks_shape[2:])]
        result = pl.pallas_call(
            functools.partial(finish_kernel, item, items, surface, pieces),
            in_specs=[on_chip()] + [whole] * (len(operands) - 1),
            out_specs=[whole] * (5 if first else 1),
            out_shape=out_shape + ([halves(order)] * 4 if first else []),
            scratch_shapes=[float_vmem(pair)] + ([float_vmem(order)] if first else []),
            compiler_params=params,
            cost_estimate=pl.CostEstimate(flops=2 * inverse_flops, bytes_accessed=0, transcendentals=0),
            name=f"finish{item}",
        )(*operands)
        greens.append(result[0])
        if first:
            sides = list(result[1:])
    return greens[-1]


def body(
    hamiltonian,
    coupling,
    self_energy,
    pattern,
    momentum_table,
    momentum_weights,
    mode_strengths,
    mode_offsets,
):
    orbitals = hamiltonian.shape[-1]
    surface = coupling.shape[-1]
    energies_here = self_energy.shape[1]
    momenta_here = self_energy.shape[2]
    energy_groups = lax.axis_size("energy")
    momentum_groups = lax.axis_size("mom")
    position = lax.axis_index("space")
    energies_all = energies_here * energy_groups
    momenta_all = momenta_here * momentum_groups
    items = energies_here * momenta_here
    branches = mode_offsets.shape[0]
    energy_index = lax.axis_index("energy") * energies_here + jnp.arange(energies_here, dtype=jnp.int32)
    momentum_index = lax.axis_index("mom") * momenta_here + jnp.arange(momenta_here, dtype=jnp.int32)
    energy = -2.0 + 4.0 * energy_index.astype(jnp.float32) / energies_all
    angle = 2.0 * jnp.pi * momentum_index.astype(jnp.float32) / momenta_all
    kinetic = dispersion * (1.0 - jnp.cos(angle))
    shift = (energy[:, None] - kinetic[None, :]).reshape(items)
    self_blocks = self_energy.reshape(items, parts, orbitals, orbitals)
    per_energy, piece_rows, pieces = row_pieces(orbitals, energy_groups, momentum_groups)
    blocks_shape = (len(pieces), items, piece_rows, orbitals)
    if lax.axis_size("space") == 2:
        green = green_two_slices(hamiltonian, coupling, self_blocks, shift, position, pieces, blocks_shape)
    else:
        slices = lax.axis_size("space")
        green = green_by_sweeps(hamiltonian[0], coupling[0], self_blocks, shift, position, slices)
        green = cut_pieces(green, pieces)

    everyone = ("energy", "mom")
    coefficients = momentum_coefficients(momentum_table, momentum_weights)
    mask_rows = jnp.concatenate([pattern[0]] * parts, axis=0)
    mask_rows = lax.dynamic_slice_in_dim(mask_rows, lax.axis_index("mom") * piece_rows, piece_rows, 0)
    green, coefficients, mask_rows, mode_offsets, mode_strengths = lax.optimization_barrier(
        (green, coefficients, mask_rows, mode_offsets, mode_strengths)
    )
    gathered = lax.all_to_all(green, everyone, split_axis=0, concat_axis=0, tiled=True)
    scattered = pl.pallas_call(
        functools.partial(
            scatter_kernel, energies_all, momenta_all, energies_here, momenta_here, momentum_groups, branches
        ),
        in_specs=[on_chip(), on_chip(), on_chip(), pl.BlockSpec(), pl.BlockSpec()],
        out_shape=jax.ShapeDtypeStruct(blocks_shape, jnp.float32),
        scratch_shapes=[float_vmem((energies_all + 1, momenta_all, piece_rows, orbitals))],
        compiler_params=pltpu.CompilerParams(vmem_limit_bytes=kernel_memory),
        name="scatter",
    )(mode_offsets, mode_strengths, coefficients, mask_rows, gathered)
    returned = lax.all_to_all(scattered, everyone, split_axis=0, concat_axis=0, tiled=True)
    returned = returned.reshape(energy_groups, momentum_groups, items, piece_rows, orbitals)
    returned = returned.transpose(2, 0, 1, 3, 4).reshape(items, energy_groups, parts, per_energy, orbitals)
    returned = returned.transpose(0, 2, 1, 3, 4)
    return returned.reshape(1, energies_here, momenta_here, parts, orbitals, orbitals)


def solution(mesh):
    return jax.shard_map(
        body,
        mesh=mesh,
        in_specs=(
            P("space", None, None),
            P("space", None, None),
            P("space", "energy", "mom", None, None, None),
            P("space", "energy", None),
            P(),
            P(),
            P(),
            P(),
        ),
        out_specs=P("space", "energy", "mom", None, None, None),
        check_vma=False,
    )
```

```python
import functools

import jax
import jax.numpy as jnp
import numpy as np
from jax import lax
from jax.experimental import pallas as pl
from jax.experimental.pallas import tpu as pltpu
from jax.sharding import PartitionSpec as P

broadening = 1.0
contact = 1.0
dispersion = 1.0
parts = 2
kernel_memory = 24 * 1024 * 1024
member_seed = 29


def split_pair(value):
    high = value.astype(jnp.bfloat16)
    return high, (value - high.astype(jnp.float32)).astype(jnp.bfloat16)


def product(left_pair, right_pair):
    left_high, left_low = left_pair
    right_high, right_low = right_pair
    dot = functools.partial(jnp.dot, preferred_element_type=jnp.float32)
    return dot(left_high, right_high) + dot(left_high, right_low) + dot(left_low, right_high)


def diagonal_mask(order_size):
    rows = lax.broadcasted_iota(jnp.int32, (order_size, order_size), 0)
    columns = lax.broadcasted_iota(jnp.int32, (order_size, order_size), 1)
    return rows == columns


def product_stacked(left_pairs, right_pair):
    rows = left_pairs[0][0].shape[0]
    count = len(left_pairs)
    right_high, right_low = right_pair
    highs = [pair[0] for pair in left_pairs]
    lows = [pair[1] for pair in left_pairs]
    dot = functools.partial(jnp.dot, preferred_element_type=jnp.float32)
    with_high = dot(jnp.concatenate(highs + lows, axis=0), right_high)
    with_low = dot(jnp.concatenate(highs, axis=0), right_low)
    return [
        with_high[i * rows : (i + 1) * rows]
        + with_high[(count + i) * rows : (count + i + 1) * rows]
        + with_low[i * rows : (i + 1) * rows]
        for i in range(count)
    ]


def inverse_pair(real_part, imag_part):
    order_size = real_part.shape[-1]
    on_diagonal = diagonal_mask(order_size)
    diag_real = jnp.sum(jnp.where(on_diagonal, real_part, 0.0), axis=0, keepdims=True)
    diag_imag = jnp.sum(jnp.where(on_diagonal, imag_part, 0.0), axis=0, keepdims=True)
    modulus = diag_real * diag_real + diag_imag * diag_imag
    column_real = diag_real / modulus
    column_imag = -diag_imag / modulus
    row_real = jnp.sum(jnp.where(on_diagonal, column_real, 0.0), axis=1, keepdims=True)
    row_imag = jnp.sum(jnp.where(on_diagonal, column_imag, 0.0), axis=1, keepdims=True)
    off_real = jnp.where(on_diagonal, 0.0, real_part)
    off_imag = jnp.where(on_diagonal, 0.0, imag_part)
    scaled_real = row_real * off_real - row_imag * off_imag
    scaled_imag = row_real * off_imag + row_imag * off_real
    pair_real = split_pair(scaled_real)
    pair_imag = split_pair(scaled_imag)
    pair_both = split_pair(scaled_real + scaled_imag)
    (square_real,) = product_stacked([pair_real], pair_real)
    (square_imag,) = product_stacked([pair_imag], pair_imag)
    (square_both,) = product_stacked([pair_both], pair_both)
    series_real = square_real - square_imag - scaled_real + jnp.where(on_diagonal, 1.0, 0.0)
    series_imag = square_both - square_real - square_imag - scaled_imag
    return (
        series_real * column_real - series_imag * column_imag,
        series_real * column_imag + series_imag * column_real,
    )


def start_kernel(item, items, surface, slice_ref, shift_ref, base_from_ref, term_from_ref, *rest):
    slice_now = slice_ref[0]
    if item == 0:
        self_from_ref, known_ref, face_ref, base_ref, term_ref = rest[:5]
        later_refs = rest[5 : 4 + items]
        self_ref, green_ref, base_buffer, coupling_buffer, wide_ref, semaphores = rest[4 + items :]
        self_copies = []
        for place, target_ref in enumerate((self_ref,) + later_refs):
            for part in range(parts):
                semaphore = semaphores.at[2 + place * parts + part]
                copy = pltpu.make_async_copy(self_from_ref.at[place, part], target_ref.at[part], semaphore)
                self_copies.append(copy)
        coupling_copy = pltpu.make_async_copy(term_from_ref.at[0], coupling_buffer, semaphores.at[0])
        base_copy = pltpu.make_async_copy(base_from_ref.at[0], base_buffer, semaphores.at[1])
        for copy in [coupling_copy, base_copy] + self_copies:
            copy.start()
    else:
        self_ref, known_ref, face_ref, green_ref = rest
        base_ref, term_ref = base_from_ref, term_from_ref
    order_size = known_ref.shape[-1]
    corner = order_size - surface
    on_diagonal = diagonal_mask(order_size)
    if item == 0:
        coupling_copy.wait()
        face_ref[parts] = jnp.zeros(face_ref.shape[1:], jnp.float32)
        face_ref[parts, :, :surface] = coupling_buffer[...]

        @pl.when(slice_now == 0)
        def _():
            rows = lax.broadcasted_iota(jnp.int32, (order_size, order_size), 0)
            inside = jnp.logical_and(on_diagonal, rows < surface)
            term_ref[...] = jnp.where(inside, contact, 0.0)

        @pl.when(slice_now != 0)
        def _():
            wide_ref[...] = jnp.zeros_like(wide_ref)
            wide_ref[corner:, :surface] = coupling_buffer[...]
            wide = wide_ref[...]
            term_ref[...] = contact * product(split_pair(wide), split_pair(wide.T))

        base_copy.wait()
        base_ref[...] = 0.5 * (base_buffer[...] + base_buffer[...].T)
        for copy in self_copies[:parts]:
            copy.wait()
    real_part = jnp.where(on_diagonal, shift_ref[item], 0.0) - base_ref[...] - self_ref[0]
    imag_part = jnp.where(on_diagonal, broadening, 0.0) - self_ref[1] + term_ref[...]
    known_ref[0] = real_part
    known_ref[1] = imag_part
    green_real, green_imag = inverse_pair(real_part, imag_part)
    green_ref[0] = green_real
    green_ref[1] = green_imag
    first = pl.multiple_of(jnp.where(slice_now == 0, corner, 0), 8)
    face_ref[:parts] = green_ref[:, pl.ds(first, surface), :]
    if item == 0:
        for copy in self_copies[parts:]:
            copy.wait()


def finish_kernel(item, items, surface, pieces, *refs):
    last = item == items - 1
    slice_ref, known_ref, face_ref = refs[:3]
    refs = refs[3:]
    if item == 0:
        own_ref, refs = refs[0], refs[1:]
    else:
        sides, refs = refs[:4], refs[4:]
    earlier_refs, refs = (refs[:item], refs[item:]) if last else ((), refs)
    out_ref, refs = refs[0], refs[1:]
    if item == 0:
        sides, refs = refs[:4], refs[4:]
    side_high_ref, side_low_ref, across_high_ref, across_low_ref = sides
    face_full_ref = refs[0]
    if item == 0:
        wide_ref = refs[1]
    order_size = known_ref.shape[-1]
    corner = order_size - surface
    slice_now = slice_ref[0]
    face_full_ref[...] = jnp.zeros_like(face_full_ref)
    if item == 0:
        wide_ref[...] = jnp.zeros_like(wide_ref)

        @pl.when(slice_now == 0)
        def _():
            wide_ref[corner:, :surface] = own_ref[parts, :, :surface]
            plain = wide_ref[...]
            side_high_ref[...], side_low_ref[...] = split_pair(plain)
            across_high_ref[...], across_low_ref[...] = split_pair(plain.T)

        @pl.when(slice_now != 0)
        def _():
            wide_ref[corner:, :surface] = face_ref[parts, :, :surface]
            plain = wide_ref[...]
            side_high_ref[...], side_low_ref[...] = split_pair(plain.T)
            across_high_ref[...], across_low_ref[...] = split_pair(plain)

    first = pl.multiple_of(jnp.where(slice_now == 0, 0, corner), 8)
    face_full_ref[:, pl.ds(first, surface), :] = face_ref[:parts]
    side = (side_high_ref[...], side_low_ref[...])
    across = (across_high_ref[...], across_low_ref[...])
    (through_real,) = product_stacked([side], split_pair(face_full_ref[0]))
    (through_imag,) = product_stacked([side], split_pair(face_full_ref[1]))
    term_real, term_imag = product_stacked([split_pair(through_real), split_pair(through_imag)], across)
    green = inverse_pair(known_ref[0] - term_real, known_ref[1] - term_imag)
    for piece, segments in enumerate(pieces):
        filled = 0
        for part, row, count in segments:
            target = (piece, item) if last else (piece,)
            out_ref[target + (slice(filled, filled + count), slice(None))] = green[part][row : row + count, :]
            filled += count
    for place, earlier_ref in enumerate(earlier_refs):
        out_ref[:, place] = earlier_ref[...]


def scatter_kernel(
    energies_all, momenta_all, energies_here, momenta_here, momentum_groups, branches, slots,
    offset_ref, strength_ref, coefficient_ref, mask_ref, in_ref, out_ref, mixed_ref,
):
    def place(energy, momentum):
        group = (energy // energies_here) * momentum_groups + momentum // momenta_here
        return slots[group], (energy % energies_here) * momenta_here + momentum % momenta_here

    mixed_ref[energies_all] = jnp.zeros(mixed_ref.shape[1:], jnp.float32)
    for energy in range(energies_all):
        blocks = [in_ref[place(energy, momentum)] for momentum in range(momenta_all)]
        for target in range(momenta_all):
            total = coefficient_ref[target, 0] * blocks[0]
            for momentum in range(1, momenta_all):
                total = total + coefficient_ref[target, momentum] * blocks[momentum]
            mixed_ref[energy, target] = total
    mask = mask_ref[...].astype(jnp.float32)
    for energy in range(energies_all):
        sources = []
        for branch in range(branches):
            below = energy - offset_ref[branch]
            above = energy + offset_ref[branch]
            below = jnp.where(jnp.logical_and(below >= 0, below < energies_all), below, energies_all)
            above = jnp.where(jnp.logical_and(above >= 0, above < energies_all), above, energies_all)
            sources.append((strength_ref[branch], below, above))
        for target in range(momenta_all):
            total = None
            for strength, below, above in sources:
                term = strength * (mixed_ref[below, target] + mixed_ref[above, target])
                total = term if total is None else total + term
            out_ref[place(energy, target)] = total * mask


def assemble_kernel(pieces, in_ref, out_ref, semaphores):
    copies = []
    for item in range(out_ref.shape[0]):
        for slot, segments in enumerate(pieces):
            filled = 0
            for part, row, count in segments:
                source = in_ref.at[slot, item, pl.ds(filled, count)]
                target = out_ref.at[item, part, pl.ds(row, count)]
                copies.append(pltpu.make_async_copy(source, target, semaphores.at[len(copies)]))
                filled += count
    for copy in copies:
        copy.start()
    for copy in copies:
        copy.wait()


def member_order(count):
    return [int(member) for member in np.random.RandomState(member_seed).permutation(count)]


def row_pieces(order_size, energy_groups, momentum_groups):
    per_energy = order_size // energy_groups
    piece_rows = parts * per_energy // momentum_groups
    pieces = []
    for energy_group in range(energy_groups):
        for momentum_group in range(momentum_groups):
            start, left, segments = momentum_group * piece_rows, piece_rows, []
            while left:
                part, inside = divmod(start, per_energy)
                count = min(left, per_energy - inside)
                segments.append((part, energy_group * per_energy + inside, count))
                start, left = start + count, left - count
            pieces.append(segments)
    return piece_rows, pieces


def momentum_coefficients(momentum_table, momentum_weights):
    momentum_count = momentum_table.shape[0]
    labels = jnp.arange(momentum_count, dtype=jnp.int32)
    matches = momentum_table[:, :, None] == labels[None, None, :]
    return jnp.sum(jnp.where(matches, momentum_weights[None, :, None], 0.0), axis=1)


def product_split(left_side, right_side):
    return product(split_pair(left_side), split_pair(right_side))


def green_by_sweeps(hamiltonian, coupling, self_blocks, shift, position, slices):
    orbitals, surface = hamiltonian.shape[-1], coupling.shape[-1]
    corner = orbitals - surface
    identity = jnp.eye(orbitals, dtype=jnp.float32)
    symmetric = 0.5 * (hamiltonian + hamiltonian.T)
    system = jnp.stack(
        [
            shift[:, None, None] * identity - symmetric - self_blocks[:, 0],
            broadening * identity - self_blocks[:, 1],
        ],
        axis=1,
    )
    source = jnp.stack([jnp.zeros((surface, surface)), -contact * jnp.eye(surface)]).astype(jnp.float32)
    source = jnp.broadcast_to(source, (system.shape[0],) + source.shape)
    over_parts = jax.vmap(jax.vmap(product_split, (None, 0)), (None, 0))
    over_parts_right = jax.vmap(jax.vmap(product_split, (0, None)), (0, None))
    around = ((0, 0), (0, 0))

    def less_first(matrix, term):
        return matrix - jnp.pad(term, around + ((0, corner), (0, corner)))

    def less_last(matrix, term):
        return matrix - jnp.pad(term, around + ((corner, 0), (corner, 0)))

    def inverse(matrix):
        return jnp.stack(jax.vmap(inverse_pair)(matrix[:, 0], matrix[:, 1]), axis=1)

    def through(side, middle):
        return over_parts_right(over_parts(side, middle), side.T)

    left = source
    right = through(coupling, source)
    for turn in range(slices - 1):
        face = inverse(less_first(system, left))[..., corner:, corner:]
        moved = lax.ppermute(through(coupling.T, face), "space", [(i, i + 1) for i in range(slices - 1)])
        left = jnp.where(position == turn + 1, moved, left)
        face = inverse(less_last(system, right))[..., :surface, :surface]
        moved = lax.ppermute(face, "space", [(i + 1, i) for i in range(slices - 1)])
        right = jnp.where(position == slices - 2 - turn, through(coupling, moved), right)
    return inverse(less_last(less_first(system, left), right))


def cut_pieces(green, pieces):
    return jnp.stack(
        [
            jnp.concatenate([green[:, part, row : row + count] for part, row, count in segments], axis=1)
            for segments in pieces
        ]
    )


def on_chip(*block):
    return pl.BlockSpec(memory_space=pltpu.SMEM)


float_vmem = functools.partial(pltpu.VMEM, dtype=jnp.float32)


def green_two_slices(hamiltonian, coupling, self_blocks, shift, position, pieces, blocks_shape):
    orbitals, surface = hamiltonian.shape[-1], coupling.shape[-1]
    items = self_blocks.shape[0]
    slice_now = position.astype(jnp.int32).reshape(1)
    order = (orbitals, orbitals)
    pair = (parts,) + order
    floats = functools.partial(jax.ShapeDtypeStruct, dtype=jnp.float32)
    halves = functools.partial(jax.ShapeDtypeStruct, dtype=jnp.bfloat16)
    whole = pl.BlockSpec(memory_space=pltpu.VMEM)
    far = pl.BlockSpec(memory_space=pltpu.HBM)
    params = pltpu.CompilerParams(vmem_limit_bytes=kernel_memory)
    inverse_flops = 18 * orbitals**3
    swap = [(0, 1), (1, 0)]

    self_blocks, base, term = (
        pltpu.with_memory_space_constraint(array, pltpu.HBM) for array in (self_blocks, hamiltonian, coupling)
    )
    known, faces, sent = [], [], []
    later = []
    for item in range(items):
        first = item == 0
        scratch = [float_vmem(pair)]
        if first:
            scratch += [float_vmem(pair), float_vmem(order), float_vmem((surface, surface)), float_vmem(order)]
            scratch += [pltpu.SemaphoreType.DMA((2 + items * parts,))]
        extra_shapes = [floats(order), floats(order)] + [floats(pair)] * (items - 1) if first else []
        result = pl.pallas_call(
            functools.partial(start_kernel, item, items, surface),
            in_specs=[on_chip(), on_chip()] + [far if first else whole] * 3,
            out_specs=[whole] * (2 + len(extra_shapes)),
            out_shape=[floats(pair), floats((parts + first, surface, orbitals))] + extra_shapes,
            scratch_shapes=scratch,
            compiler_params=params,
            cost_estimate=pl.CostEstimate(flops=inverse_flops, bytes_accessed=0, transcendentals=0),
            name=f"start{item}",
        )(slice_now, shift, base, term, self_blocks if first else later[item - 1])
        known.append(result[0])
        if first:
            base, term, *later = result[2:]
        sent.append(result[1])
        faces.append(lax.ppermute(result[1], "space", swap))

    greens, sides = [], []
    for item in range(items):
        first, last = item == 0, item == items - 1
        operands = [slice_now, known[item], faces[item]] + ([sent[item]] if first else sides) + (greens if last else [])
        out_shape = [floats(blocks_shape if last else blocks_shape[:1] + blocks_shape[2:])]
        result = pl.pallas_call(
            functools.partial(finish_kernel, item, items, surface, pieces),
            in_specs=[on_chip()] + [whole] * (len(operands) - 1),
            out_specs=[whole] * (5 if first else 1),
            out_shape=out_shape + ([halves(order)] * 4 if first else []),
            scratch_shapes=[float_vmem(pair)] + ([float_vmem(order)] if first else []),
            compiler_params=params,
            cost_estimate=pl.CostEstimate(flops=2 * inverse_flops, bytes_accessed=0, transcendentals=0),
            name=f"finish{item}",
        )(*operands)
        greens.append(result[0])
        if first:
            sides = list(result[1:])
    return greens[-1]


def body(
    hamiltonian,
    coupling,
    self_energy,
    pattern,
    momentum_table,
    momentum_weights,
    mode_strengths,
    mode_offsets,
):
    orbitals = hamiltonian.shape[-1]
    surface = coupling.shape[-1]
    energies_here = self_energy.shape[1]
    momenta_here = self_energy.shape[2]
    energy_groups = lax.axis_size("energy")
    momentum_groups = lax.axis_size("mom")
    position = lax.axis_index("space")
    energies_all = energies_here * energy_groups
    momenta_all = momenta_here * momentum_groups
    items = energies_here * momenta_here
    branches = mode_offsets.shape[0]
    energy_index = lax.axis_index("energy") * energies_here + jnp.arange(energies_here, dtype=jnp.int32)
    momentum_index = lax.axis_index("mom") * momenta_here + jnp.arange(momenta_here, dtype=jnp.int32)
    energy = -2.0 + 4.0 * energy_index.astype(jnp.float32) / energies_all
    angle = 2.0 * jnp.pi * momentum_index.astype(jnp.float32) / momenta_all
    kinetic = dispersion * (1.0 - jnp.cos(angle))
    shift = (energy[:, None] - kinetic[None, :]).reshape(items)
    self_blocks = self_energy.reshape(items, parts, orbitals, orbitals)
    piece_rows, pieces = row_pieces(orbitals, energy_groups, momentum_groups)
    members = member_order(len(pieces))
    slots = [members.index(group) for group in range(len(members))]
    pieces = [pieces[member] for member in members]
    blocks_shape = (len(pieces), items, piece_rows, orbitals)
    if lax.axis_size("space") == 2:
        green = green_two_slices(hamiltonian, coupling, self_blocks, shift, position, pieces, blocks_shape)
    else:
        slices = lax.axis_size("space")
        green = green_by_sweeps(hamiltonian[0], coupling[0], self_blocks, shift, position, slices)
        green = cut_pieces(green, pieces)

    exchange = functools.partial(
        lax.all_to_all,
        axis_name=("energy", "mom"),
        split_axis=0,
        concat_axis=0,
        axis_index_groups=[members],
        tiled=True,
    )
    coefficients = momentum_coefficients(momentum_table, momentum_weights)
    mask_rows = jnp.concatenate([pattern[0]] * parts, axis=0)
    mask_rows = lax.dynamic_slice_in_dim(mask_rows, lax.axis_index("mom") * piece_rows, piece_rows, 0)
    green, coefficients, mask_rows, mode_offsets, mode_strengths = lax.optimization_barrier(
        (green, coefficients, mask_rows, mode_offsets, mode_strengths)
    )
    gathered = exchange(green)
    scattered = pl.pallas_call(
        functools.partial(
            scatter_kernel, energies_all, momenta_all, energies_here, momenta_here, momentum_groups, branches, slots
        ),
        in_specs=[on_chip(), on_chip(), on_chip(), pl.BlockSpec(), pl.BlockSpec()],
        out_shape=jax.ShapeDtypeStruct(blocks_shape, jnp.float32),
        scratch_shapes=[float_vmem((energies_all + 1, momenta_all, piece_rows, orbitals))],
        compiler_params=pltpu.CompilerParams(vmem_limit_bytes=kernel_memory),
        name="scatter",
    )(mode_offsets, mode_strengths, coefficients, mask_rows, gathered)
    returned = exchange(scattered)
    copies = items * sum(len(segments) for segments in pieces)
    whole = pl.pallas_call(
        functools.partial(assemble_kernel, pieces),
        in_specs=[pl.BlockSpec(memory_space=pltpu.VMEM)],
        out_specs=pl.BlockSpec(memory_space=pltpu.HBM),
        out_shape=jax.ShapeDtypeStruct((items, parts, orbitals, orbitals), jnp.float32),
        scratch_shapes=[pltpu.SemaphoreType.DMA((copies,))],
        compiler_params=pltpu.CompilerParams(vmem_limit_bytes=kernel_memory),
        name="assemble",
    )(returned)
    return whole.reshape(1, energies_here, momenta_here, parts, orbitals, orbitals)


def solution(mesh):
    return jax.shard_map(
        body,
        mesh=mesh,
        in_specs=(
            P("space", None, None),
            P("space", None, None),
            P("space", "energy", "mom", None, None, None),
            P("space", "energy", None),
            P(),
            P(),
            P(),
            P(),
        ),
        out_specs=P("space", "energy", "mom", None, None, None),
        check_vma=False,
    )
```

```python
import functools

import jax
import jax.numpy as jnp
import numpy as np
from jax import lax
from jax.experimental import pallas as pl
from jax.experimental.pallas import tpu as pltpu
from jax.sharding import PartitionSpec as P

broadening = 1.0
contact = 1.0
dispersion = 1.0
parts = 2
kernel_memory = 24 * 1024 * 1024
member_seed = 117


def split_pair(value):
    high = value.astype(jnp.bfloat16)
    return high, (value - high.astype(jnp.float32)).astype(jnp.bfloat16)


def product(left_pair, right_pair):
    left_high, left_low = left_pair
    right_high, right_low = right_pair
    dot = functools.partial(jnp.dot, preferred_element_type=jnp.float32)
    return dot(left_high, right_high) + dot(left_high, right_low) + dot(left_low, right_high)


def diagonal_mask(order_size):
    rows = lax.broadcasted_iota(jnp.int32, (order_size, order_size), 0)
    columns = lax.broadcasted_iota(jnp.int32, (order_size, order_size), 1)
    return rows == columns


def product_stacked(left_pairs, right_pair):
    rows = left_pairs[0][0].shape[0]
    count = len(left_pairs)
    right_high, right_low = right_pair
    highs = [pair[0] for pair in left_pairs]
    lows = [pair[1] for pair in left_pairs]
    dot = functools.partial(jnp.dot, preferred_element_type=jnp.float32)
    with_high = dot(jnp.concatenate(highs + lows, axis=0), right_high)
    with_low = dot(jnp.concatenate(highs, axis=0), right_low)
    return [
        with_high[i * rows : (i + 1) * rows]
        + with_high[(count + i) * rows : (count + i + 1) * rows]
        + with_low[i * rows : (i + 1) * rows]
        for i in range(count)
    ]


def inverse_pair(real_part, imag_part):
    order_size = real_part.shape[-1]
    on_diagonal = diagonal_mask(order_size)
    diag_real = jnp.sum(jnp.where(on_diagonal, real_part, 0.0), axis=0, keepdims=True)
    diag_imag = jnp.sum(jnp.where(on_diagonal, imag_part, 0.0), axis=0, keepdims=True)
    modulus = diag_real * diag_real + diag_imag * diag_imag
    column_real = diag_real / modulus
    column_imag = -diag_imag / modulus
    row_real = jnp.sum(jnp.where(on_diagonal, column_real, 0.0), axis=1, keepdims=True)
    row_imag = jnp.sum(jnp.where(on_diagonal, column_imag, 0.0), axis=1, keepdims=True)
    off_real = jnp.where(on_diagonal, 0.0, real_part)
    off_imag = jnp.where(on_diagonal, 0.0, imag_part)
    scaled_real = row_real * off_real - row_imag * off_imag
    scaled_imag = row_real * off_imag + row_imag * off_real
    pair_real = split_pair(scaled_real)
    pair_imag = split_pair(scaled_imag)
    pair_both = split_pair(scaled_real + scaled_imag)
    (square_real,) = product_stacked([pair_real], pair_real)
    (square_imag,) = product_stacked([pair_imag], pair_imag)
    (square_both,) = product_stacked([pair_both], pair_both)
    series_real = square_real - square_imag - scaled_real + jnp.where(on_diagonal, 1.0, 0.0)
    series_imag = square_both - square_real - square_imag - scaled_imag
    return (
        series_real * column_real - series_imag * column_imag,
        series_real * column_imag + series_imag * column_real,
    )


def write_factors(factor_ref, table_ref, weight_ref, strength_ref, offset_ref):
    momenta_all, branches = weight_ref.shape[0], strength_ref.shape[0]
    values = []
    for target in range(momenta_all):
        for source in range(momenta_all):
            total = jnp.float32(0.0)
            for transfer in range(momenta_all):
                total += jnp.where(table_ref[target, transfer] == source, weight_ref[transfer], 0.0)
            values.append(total)
    values += [strength_ref[branch] for branch in range(branches)]
    values += [offset_ref[branch].astype(jnp.float32) for branch in range(branches)]
    for place, value in enumerate(values):
        factor_ref[place] = jnp.full(factor_ref.shape[1:], value, jnp.float32)


def start_kernel(item, items, surface, slice_ref, shift_ref, base_from_ref, term_from_ref, *rest):
    slice_now = slice_ref[0]
    if item == 0:
        self_from_ref, small_refs = rest[0], rest[1:5]
        known_ref, face_ref, base_ref, term_ref, factor_ref = rest[5:10]
        later_refs = rest[10 : 9 + items]
        self_ref, base_buffer, coupling_buffer, wide_ref = rest[9 + items : 13 + items]
        near_refs, semaphores, small_semaphores = rest[13 + items : 17 + items], rest[-2], rest[-1]
        small_copies = [
            pltpu.make_async_copy(small_ref, near_ref, small_semaphores.at[place])
            for place, (small_ref, near_ref) in enumerate(zip(small_refs, near_refs))
        ]
        self_copies = []
        for place, target_ref in enumerate((self_ref,) + later_refs):
            for part in range(parts):
                semaphore = semaphores.at[2 + place * parts + part]
                copy = pltpu.make_async_copy(self_from_ref.at[place, part], target_ref.at[part], semaphore)
                self_copies.append(copy)
        coupling_copy = pltpu.make_async_copy(term_from_ref.at[0], coupling_buffer, semaphores.at[0])
        base_copy = pltpu.make_async_copy(base_from_ref.at[0], base_buffer, semaphores.at[1])
        for copy in [coupling_copy, base_copy] + self_copies[:parts] + small_copies + self_copies[parts:]:
            copy.start()
    else:
        self_ref, known_ref, face_ref = rest
        base_ref, term_ref = base_from_ref, term_from_ref
    order_size = known_ref.shape[-1]
    corner = order_size - surface
    on_diagonal = diagonal_mask(order_size)
    if item == 0:
        coupling_copy.wait()
        face_ref[parts] = jnp.zeros(face_ref.shape[1:], jnp.float32)
        face_ref[parts, :, :surface] = coupling_buffer[...]

        @pl.when(slice_now == 0)
        def _():
            rows = lax.broadcasted_iota(jnp.int32, (order_size, order_size), 0)
            inside = jnp.logical_and(on_diagonal, rows < surface)
            term_ref[...] = jnp.where(inside, contact, 0.0)

        @pl.when(slice_now != 0)
        def _():
            wide_ref[...] = jnp.zeros_like(wide_ref)
            wide_ref[corner:, :surface] = coupling_buffer[...]
            wide = wide_ref[...]
            term_ref[...] = contact * product(split_pair(wide), split_pair(wide.T))

        base_copy.wait()
        base_ref[...] = 0.5 * (base_buffer[...] + base_buffer[...].T)
        for copy in self_copies[:parts]:
            copy.wait()
    real_part = jnp.where(on_diagonal, shift_ref[item], 0.0) - base_ref[...] - self_ref[0]
    imag_part = jnp.where(on_diagonal, broadening, 0.0) - self_ref[1] + term_ref[...]
    known_ref[0] = real_part
    known_ref[1] = imag_part
    green_real, green_imag = inverse_pair(real_part, imag_part)

    @pl.when(slice_now == 0)
    def _():
        face_ref[0] = green_real[corner:]
        face_ref[1] = green_imag[corner:]

    @pl.when(slice_now != 0)
    def _():
        face_ref[0] = green_real[:surface]
        face_ref[1] = green_imag[:surface]

    if item == 0:
        for copy in small_copies + self_copies[parts:]:
            copy.wait()
        write_factors(factor_ref, *near_refs)


def finish_kernel(item, items, surface, pieces, *refs):
    last = item == items - 1
    slice_ref, known_ref, face_ref = refs[:3]
    refs = refs[3:]
    if item == 0:
        own_ref, refs = refs[0], refs[1:]
    else:
        sides, refs = refs[:4], refs[4:]
    earlier_refs, refs = (refs[:item], refs[item:]) if last else ((), refs)
    out_ref, refs = refs[0], refs[1:]
    if item == 0:
        sides, refs = refs[:4], refs[4:]
    side_high_ref, side_low_ref, across_high_ref, across_low_ref = sides
    if item == 0:
        wide_ref = refs[0]
    order_size = known_ref.shape[-1]
    corner = order_size - surface
    slice_now = slice_ref[0]
    if item == 0:
        wide_ref[...] = jnp.zeros_like(wide_ref)

        @pl.when(slice_now == 0)
        def _():
            wide_ref[corner:, :surface] = own_ref[parts, :, :surface]
            plain = wide_ref[...]
            side_high_ref[...], side_low_ref[...] = split_pair(plain[:, :surface])
            across_high_ref[...], across_low_ref[...] = split_pair(plain.T)

        @pl.when(slice_now != 0)
        def _():
            wide_ref[corner:, :surface] = face_ref[parts, :, :surface]
            plain = wide_ref[...]
            side_high_ref[:surface], side_low_ref[:surface] = split_pair(face_ref[parts, :, :surface].T)
            side_high_ref[surface:] = jnp.zeros((corner, surface), jnp.bfloat16)
            side_low_ref[surface:] = jnp.zeros((corner, surface), jnp.bfloat16)
            across_high_ref[...], across_low_ref[...] = split_pair(plain)

    side = (side_high_ref[...], side_low_ref[...])
    across = (across_high_ref[...], across_low_ref[...])
    (through_real,) = product_stacked([side], split_pair(face_ref[0]))
    (through_imag,) = product_stacked([side], split_pair(face_ref[1]))
    term_real, term_imag = product_stacked([split_pair(through_real), split_pair(through_imag)], across)
    green = inverse_pair(known_ref[0] - term_real, known_ref[1] - term_imag)
    for piece, segments in enumerate(pieces):
        filled = 0
        for part, row, count in segments:
            target = (piece, item) if last else (piece,)
            out_ref[target + (slice(filled, filled + count), slice(None))] = green[part][row : row + count, :]
            filled += count
    for place, earlier_ref in enumerate(earlier_refs):
        out_ref[:, place] = earlier_ref[...]


def scatter_kernel(
    energies_all, momenta_all, energies_here, momenta_here, momentum_groups, branches, slots,
    group_ref, factor_ref, pattern_ref, in_ref, out_ref, mixed_ref,
):
    table_size = momenta_all * momenta_all
    offsets = [jnp.max(factor_ref[table_size + branches + branch]).astype(jnp.int32) for branch in range(branches)]

    def place(energy, momentum):
        group = (energy // energies_here) * momentum_groups + momentum // momenta_here
        return slots[group], (energy % energies_here) * momenta_here + momentum % momenta_here

    piece_rows = in_ref.shape[2]
    per_energy = pattern_ref.shape[1]
    if piece_rows <= per_energy:
        first = lax.rem(group_ref[0] * piece_rows, per_energy)
        mask = pattern_ref[0, pl.ds(pl.multiple_of(first, piece_rows), piece_rows), :]
    else:
        mask = jnp.concatenate([pattern_ref[0]] * (piece_rows // per_energy), axis=0)
    mask = mask.astype(jnp.float32)
    mixed_ref[energies_all] = jnp.zeros(mixed_ref.shape[1:], jnp.float32)
    for energy in range(energies_all):
        blocks = [in_ref[place(energy, momentum)] for momentum in range(momenta_all)]
        for target in range(momenta_all):
            total = factor_ref[target * momenta_all] * blocks[0]
            for momentum in range(1, momenta_all):
                total = total + factor_ref[target * momenta_all + momentum] * blocks[momentum]
            mixed_ref[energy, target] = total
    for energy in range(energies_all):
        sources = []
        for branch in range(branches):
            below = energy - offsets[branch]
            above = energy + offsets[branch]
            below = jnp.where(jnp.logical_and(below >= 0, below < energies_all), below, energies_all)
            above = jnp.where(jnp.logical_and(above >= 0, above < energies_all), above, energies_all)
            sources.append((factor_ref[table_size + branch], below, above))
        for target in range(momenta_all):
            total = None
            for strength, below, above in sources:
                term = strength * (mixed_ref[below, target] + mixed_ref[above, target])
                total = term if total is None else total + term
            out_ref[place(energy, target)] = total * mask


def momentum_coefficients(momentum_table, momentum_weights):
    momentum_count = momentum_table.shape[0]
    labels = jnp.arange(momentum_count, dtype=jnp.int32)
    matches = momentum_table[:, :, None] == labels[None, None, :]
    return jnp.sum(jnp.where(matches, momentum_weights[None, :, None], 0.0), axis=1)


def assemble_kernel(pieces, in_ref, out_ref, semaphores):
    copies = []
    for item in range(out_ref.shape[0]):
        for slot, segments in enumerate(pieces):
            filled = 0
            for part, row, count in segments:
                source = in_ref.at[slot, item, pl.ds(filled, count)]
                target = out_ref.at[item, part, pl.ds(row, count)]
                copies.append(pltpu.make_async_copy(source, target, semaphores.at[len(copies)]))
                filled += count
    for copy in copies:
        copy.start()
    for copy in copies:
        copy.wait()


def member_order(count):
    return [int(member) for member in np.random.RandomState(member_seed).permutation(count)]


def row_pieces(order_size, energy_groups, momentum_groups):
    per_energy = order_size // energy_groups
    piece_rows = parts * per_energy // momentum_groups
    pieces = []
    for energy_group in range(energy_groups):
        for momentum_group in range(momentum_groups):
            start, left, segments = momentum_group * piece_rows, piece_rows, []
            while left:
                part, inside = divmod(start, per_energy)
                count = min(left, per_energy - inside)
                segments.append((part, energy_group * per_energy + inside, count))
                start, left = start + count, left - count
            pieces.append(segments)
    return piece_rows, pieces


def product_split(left_side, right_side):
    return product(split_pair(left_side), split_pair(right_side))


def green_by_sweeps(hamiltonian, coupling, self_blocks, shift, position, slices):
    orbitals, surface = hamiltonian.shape[-1], coupling.shape[-1]
    corner = orbitals - surface
    identity = jnp.eye(orbitals, dtype=jnp.float32)
    symmetric = 0.5 * (hamiltonian + hamiltonian.T)
    system = jnp.stack(
        [
            shift[:, None, None] * identity - symmetric - self_blocks[:, 0],
            broadening * identity - self_blocks[:, 1],
        ],
        axis=1,
    )
    source = jnp.stack([jnp.zeros((surface, surface)), -contact * jnp.eye(surface)]).astype(jnp.float32)
    source = jnp.broadcast_to(source, (system.shape[0],) + source.shape)
    over_parts = jax.vmap(jax.vmap(product_split, (None, 0)), (None, 0))
    over_parts_right = jax.vmap(jax.vmap(product_split, (0, None)), (0, None))
    around = ((0, 0), (0, 0))

    def less_first(matrix, term):
        return matrix - jnp.pad(term, around + ((0, corner), (0, corner)))

    def less_last(matrix, term):
        return matrix - jnp.pad(term, around + ((corner, 0), (corner, 0)))

    def inverse(matrix):
        return jnp.stack(jax.vmap(inverse_pair)(matrix[:, 0], matrix[:, 1]), axis=1)

    def through(side, middle):
        return over_parts_right(over_parts(side, middle), side.T)

    left = source
    right = through(coupling, source)
    for turn in range(slices - 1):
        face = inverse(less_first(system, left))[..., corner:, corner:]
        moved = lax.ppermute(through(coupling.T, face), "space", [(i, i + 1) for i in range(slices - 1)])
        left = jnp.where(position == turn + 1, moved, left)
        face = inverse(less_last(system, right))[..., :surface, :surface]
        moved = lax.ppermute(face, "space", [(i + 1, i) for i in range(slices - 1)])
        right = jnp.where(position == slices - 2 - turn, through(coupling, moved), right)
    return inverse(less_last(less_first(system, left), right))


def cut_pieces(green, pieces):
    return jnp.stack(
        [
            jnp.concatenate([green[:, part, row : row + count] for part, row, count in segments], axis=1)
            for segments in pieces
        ]
    )


def on_chip(*block):
    return pl.BlockSpec(memory_space=pltpu.SMEM)


float_vmem = functools.partial(pltpu.VMEM, dtype=jnp.float32)


def green_two_slices(hamiltonian, coupling, self_blocks, shift, position, pieces, blocks_shape, small):
    orbitals, surface = hamiltonian.shape[-1], coupling.shape[-1]
    items = self_blocks.shape[0]
    slice_now = position.astype(jnp.int32).reshape(1)
    order = (orbitals, orbitals)
    pair = (parts,) + order
    floats = functools.partial(jax.ShapeDtypeStruct, dtype=jnp.float32)
    halves = functools.partial(jax.ShapeDtypeStruct, dtype=jnp.bfloat16)
    whole = pl.BlockSpec(memory_space=pltpu.VMEM)
    far = pl.BlockSpec(memory_space=pltpu.HBM)
    params = pltpu.CompilerParams(vmem_limit_bytes=kernel_memory)
    inverse_flops = 18 * orbitals**3
    swap = [(0, 1), (1, 0)]

    shift = jnp.broadcast_to(shift[:, None, None], (items, 1, orbitals))
    self_blocks, base, term = (
        pltpu.with_memory_space_constraint(array, pltpu.HBM) for array in (self_blocks, hamiltonian, coupling)
    )
    small = [pltpu.with_memory_space_constraint(array, pltpu.HBM) for array in small]
    factor_count = small[0].size + small[2].size + small[3].size
    known, faces, sent = [], [], []
    later = []
    for item in range(items):
        first = item == 0
        scratch = []
        if first:
            scratch += [float_vmem(pair), float_vmem(order), float_vmem((surface, surface)), float_vmem(order)]
            scratch += [pltpu.SMEM(array.shape, array.dtype) for array in small]
            scratch += [pltpu.SemaphoreType.DMA((2 + items * parts,)), pltpu.SemaphoreType.DMA((len(small),))]
        extra_shapes = []
        if first:
            extra_shapes = [floats(order), floats(order), floats((factor_count, 1, orbitals))]
            extra_shapes += [floats(pair)] * (items - 1)
        result = pl.pallas_call(
            functools.partial(start_kernel, item, items, surface),
            in_specs=[on_chip(), whole] + ([far] * (3 + len(small)) if first else [whole] * 3),
            out_specs=[whole] * (2 + len(extra_shapes)),
            out_shape=[floats(pair), floats((parts + first, surface, orbitals))] + extra_shapes,
            scratch_shapes=scratch,
            compiler_params=params,
            cost_estimate=pl.CostEstimate(flops=inverse_flops, bytes_accessed=0, transcendentals=0),
            name=f"start{item}",
        )(slice_now, shift, base, term, *([self_blocks] + small if first else [later[item - 1]]))
        known.append(result[0])
        if first:
            base, term, factors, *later = result[2:]
        sent.append(result[1])
        faces.append(lax.ppermute(result[1], "space", swap))

    greens, sides = [], []
    for item in range(items):
        first, last = item == 0, item == items - 1
        operands = [slice_now, known[item], faces[item]] + ([sent[item]] if first else sides) + (greens if last else [])
        out_shape = [floats(blocks_shape if last else blocks_shape[:1] + blocks_shape[2:])]
        result = pl.pallas_call(
            functools.partial(finish_kernel, item, items, surface, pieces),
            in_specs=[on_chip()] + [whole] * (len(operands) - 1),
            out_specs=[whole] * (5 if first else 1),
            out_shape=out_shape + ([halves((orbitals, surface))] * 2 + [halves(order)] * 2 if first else []),
            scratch_shapes=[float_vmem(order)] if first else [],
            compiler_params=params,
            cost_estimate=pl.CostEstimate(flops=2 * inverse_flops, bytes_accessed=0, transcendentals=0),
            name=f"finish{item}",
        )(*operands)
        greens.append(result[0])
        if first:
            sides = list(result[1:])
    return greens[-1], factors


def body(
    hamiltonian,
    coupling,
    self_energy,
    pattern,
    momentum_table,
    momentum_weights,
    mode_strengths,
    mode_offsets,
):
    orbitals = hamiltonian.shape[-1]
    surface = coupling.shape[-1]
    energies_here = self_energy.shape[1]
    momenta_here = self_energy.shape[2]
    energy_groups = lax.axis_size("energy")
    momentum_groups = lax.axis_size("mom")
    position = lax.axis_index("space")
    energies_all = energies_here * energy_groups
    momenta_all = momenta_here * momentum_groups
    items = energies_here * momenta_here
    branches = mode_offsets.shape[0]
    energy_index = lax.axis_index("energy") * energies_here + jnp.arange(energies_here, dtype=jnp.int32)
    momentum_index = lax.axis_index("mom") * momenta_here + jnp.arange(momenta_here, dtype=jnp.int32)
    energy = -2.0 + 4.0 * energy_index.astype(jnp.float32) / energies_all
    angle = 2.0 * jnp.pi * momentum_index.astype(jnp.float32) / momenta_all
    kinetic = dispersion * (1.0 - jnp.cos(angle))
    shift = (energy[:, None] - kinetic[None, :]).reshape(items)
    self_blocks = self_energy.reshape(items, parts, orbitals, orbitals)
    piece_rows, pieces = row_pieces(orbitals, energy_groups, momentum_groups)
    members = member_order(len(pieces))
    slots = [members.index(group) for group in range(len(members))]
    pieces = [pieces[member] for member in members]
    blocks_shape = (len(pieces), items, piece_rows, orbitals)
    if lax.axis_size("space") == 2:
        small = (momentum_table, momentum_weights, mode_strengths, mode_offsets)
        green, factors = green_two_slices(
            hamiltonian, coupling, self_blocks, shift, position, pieces, blocks_shape, small
        )
    else:
        slices = lax.axis_size("space")
        green = green_by_sweeps(hamiltonian[0], coupling[0], self_blocks, shift, position, slices)
        green = cut_pieces(green, pieces)
        factors = momentum_coefficients(momentum_table, momentum_weights).reshape(-1)
        factors = jnp.concatenate([factors, mode_strengths, mode_offsets.astype(jnp.float32)])
        factors = jnp.broadcast_to(factors[:, None, None], (factors.shape[0], 1, orbitals))

    exchange = functools.partial(
        lax.all_to_all,
        axis_name=("energy", "mom"),
        split_axis=0,
        concat_axis=0,
        axis_index_groups=[members],
        tiled=True,
    )
    momentum_group = lax.axis_index("mom").astype(jnp.int32).reshape(1)
    gathered = exchange(green)
    scattered = pl.pallas_call(
        functools.partial(
            scatter_kernel, energies_all, momenta_all, energies_here, momenta_here, momentum_groups, branches, slots
        ),
        in_specs=[on_chip()] + [pl.BlockSpec(memory_space=pltpu.VMEM)] * 3,
        out_shape=jax.ShapeDtypeStruct(blocks_shape, jnp.float32),
        scratch_shapes=[float_vmem((energies_all + 1, momenta_all, piece_rows, orbitals))],
        compiler_params=pltpu.CompilerParams(vmem_limit_bytes=kernel_memory),
        name="scatter",
    )(momentum_group, factors, pattern, gathered)
    returned = exchange(scattered)
    copies = items * sum(len(segments) for segments in pieces)
    whole = pl.pallas_call(
        functools.partial(assemble_kernel, pieces),
        in_specs=[pl.BlockSpec(memory_space=pltpu.VMEM)],
        out_specs=pl.BlockSpec(memory_space=pltpu.HBM),
        out_shape=jax.ShapeDtypeStruct((items, parts, orbitals, orbitals), jnp.float32),
        scratch_shapes=[pltpu.SemaphoreType.DMA((copies,))],
        compiler_params=pltpu.CompilerParams(vmem_limit_bytes=kernel_memory),
        name="assemble",
    )(returned)
    return whole.reshape(1, energies_here, momenta_here, parts, orbitals, orbitals)


def solution(mesh):
    return jax.shard_map(
        body,
        mesh=mesh,
        in_specs=(
            P("space", None, None),
            P("space", None, None),
            P("space", "energy", "mom", None, None, None),
            P("space", "energy", None),
            P(),
            P(),
            P(),
            P(),
        ),
        out_specs=P("space", "energy", "mom", None, None, None),
        check_vma=False,
    )
```

```python
import functools

import jax
import jax.numpy as jnp
import numpy as np
from jax import lax
from jax.experimental import pallas as pl
from jax.experimental.pallas import tpu as pltpu
from jax.sharding import PartitionSpec as P

broadening = 1.0
contact = 1.0
dispersion = 1.0
parts = 2
kernel_memory = 24 * 1024 * 1024
member_seed = 79


def split_pair(value):
    high = value.astype(jnp.bfloat16)
    return high, (value - high.astype(jnp.float32)).astype(jnp.bfloat16)


def product(left_pair, right_pair):
    left_high, left_low = left_pair
    right_high, right_low = right_pair
    dot = functools.partial(jnp.dot, preferred_element_type=jnp.float32)
    return dot(left_high, right_high) + dot(left_high, right_low) + dot(left_low, right_high)


def diagonal_mask(order_size):
    rows = lax.broadcasted_iota(jnp.int32, (order_size, order_size), 0)
    columns = lax.broadcasted_iota(jnp.int32, (order_size, order_size), 1)
    return rows == columns


def product_stacked(left_pairs, right_pair):
    rows = left_pairs[0][0].shape[0]
    count = len(left_pairs)
    right_high, right_low = right_pair
    highs = [pair[0] for pair in left_pairs]
    lows = [pair[1] for pair in left_pairs]
    dot = functools.partial(jnp.dot, preferred_element_type=jnp.float32)
    with_high = dot(jnp.concatenate(highs + lows, axis=0), right_high)
    with_low = dot(jnp.concatenate(highs, axis=0), right_low)
    return [
        with_high[i * rows : (i + 1) * rows]
        + with_high[(count + i) * rows : (count + i + 1) * rows]
        + with_low[i * rows : (i + 1) * rows]
        for i in range(count)
    ]


def inverse_pair(real_part, imag_part):
    order_size = real_part.shape[-1]
    on_diagonal = diagonal_mask(order_size)
    diag_real = jnp.sum(jnp.where(on_diagonal, real_part, 0.0), axis=0, keepdims=True)
    diag_imag = jnp.sum(jnp.where(on_diagonal, imag_part, 0.0), axis=0, keepdims=True)
    modulus = diag_real * diag_real + diag_imag * diag_imag
    column_real = diag_real / modulus
    column_imag = -diag_imag / modulus
    row_real = jnp.sum(jnp.where(on_diagonal, column_real, 0.0), axis=1, keepdims=True)
    row_imag = jnp.sum(jnp.where(on_diagonal, column_imag, 0.0), axis=1, keepdims=True)
    off_real = jnp.where(on_diagonal, 0.0, real_part)
    off_imag = jnp.where(on_diagonal, 0.0, imag_part)
    scaled_real = row_real * off_real - row_imag * off_imag
    scaled_imag = row_real * off_imag + row_imag * off_real
    pair_real = split_pair(scaled_real)
    pair_imag = split_pair(scaled_imag)
    pair_both = split_pair(scaled_real + scaled_imag)
    (square_real,) = product_stacked([pair_real], pair_real)
    (square_imag,) = product_stacked([pair_imag], pair_imag)
    (square_both,) = product_stacked([pair_both], pair_both)
    series_real = square_real - square_imag - scaled_real + jnp.where(on_diagonal, 1.0, 0.0)
    series_imag = square_both - square_real - square_imag - scaled_imag
    return (
        series_real * column_real - series_imag * column_imag,
        series_real * column_imag + series_imag * column_real,
    )


def write_factors(factor_ref, table_ref, weight_ref, strength_ref, offset_ref):
    momenta_all, branches = weight_ref.shape[0], strength_ref.shape[0]
    values = []
    for target in range(momenta_all):
        for source in range(momenta_all):
            total = jnp.float32(0.0)
            for transfer in range(momenta_all):
                total += jnp.where(table_ref[target, transfer] == source, weight_ref[transfer], 0.0)
            values.append(total)
    values += [strength_ref[branch] for branch in range(branches)]
    values += [offset_ref[branch].astype(jnp.float32) for branch in range(branches)]
    for place, value in enumerate(values):
        factor_ref[place] = jnp.full(factor_ref.shape[1:], value, jnp.float32)


def start_kernel(item, items, surface, slice_ref, shift_ref, base_from_ref, term_from_ref, *rest):
    slice_now = slice_ref[0]
    if item == 0:
        self_from_ref, small_refs = rest[0], rest[1:5]
        known_ref, face_ref, base_ref, term_ref, factor_ref = rest[5:10]
        later_refs = rest[10 : 9 + items]
        self_ref, base_buffer, coupling_buffer, wide_ref = rest[9 + items : 13 + items]
        near_refs, semaphores, small_semaphores = rest[13 + items : 17 + items], rest[-2], rest[-1]
        small_copies = [
            pltpu.make_async_copy(small_ref, near_ref, small_semaphores.at[place])
            for place, (small_ref, near_ref) in enumerate(zip(small_refs, near_refs))
        ]
        self_copies = []
        for place, target_ref in enumerate((self_ref,) + later_refs):
            for part in range(parts):
                semaphore = semaphores.at[2 + place * parts + part]
                copy = pltpu.make_async_copy(self_from_ref.at[place, part], target_ref.at[part], semaphore)
                self_copies.append(copy)
        coupling_copy = pltpu.make_async_copy(term_from_ref.at[0], coupling_buffer, semaphores.at[0])
        base_copy = pltpu.make_async_copy(base_from_ref.at[0], base_buffer, semaphores.at[1])
        for copy in [coupling_copy, base_copy] + self_copies[:parts] + small_copies + self_copies[parts:]:
            copy.start()
    else:
        self_ref, known_ref, face_ref = rest
        base_ref, term_ref = base_from_ref, term_from_ref
    order_size = known_ref.shape[-1]
    corner = order_size - surface
    on_diagonal = diagonal_mask(order_size)
    if item == 0:
        coupling_copy.wait()
        face_ref[parts] = jnp.zeros(face_ref.shape[1:], jnp.float32)
        face_ref[parts, :, :surface] = coupling_buffer[...]

        @pl.when(slice_now == 0)
        def _():
            rows = lax.broadcasted_iota(jnp.int32, (order_size, order_size), 0)
            inside = jnp.logical_and(on_diagonal, rows < surface)
            term_ref[...] = jnp.where(inside, contact, 0.0)

        @pl.when(slice_now != 0)
        def _():
            wide_ref[...] = jnp.zeros_like(wide_ref)
            wide_ref[corner:, :surface] = coupling_buffer[...]
            wide = wide_ref[...]
            term_ref[...] = contact * product(split_pair(wide), split_pair(wide.T))

        base_copy.wait()
        base_ref[...] = 0.5 * (base_buffer[...] + base_buffer[...].T)
        for copy in self_copies[:parts]:
            copy.wait()
    real_part = jnp.where(on_diagonal, shift_ref[item], 0.0) - base_ref[...] - self_ref[0]
    imag_part = jnp.where(on_diagonal, broadening, 0.0) - self_ref[1] + term_ref[...]
    known_ref[0] = real_part
    known_ref[1] = imag_part
    green_real, green_imag = inverse_pair(real_part, imag_part)

    @pl.when(slice_now == 0)
    def _():
        face_ref[0] = green_real[corner:]
        face_ref[1] = green_imag[corner:]

    @pl.when(slice_now != 0)
    def _():
        face_ref[0] = green_real[:surface]
        face_ref[1] = green_imag[:surface]

    if item == 0:
        for copy in small_copies + self_copies[parts:]:
            copy.wait()
        write_factors(factor_ref, *near_refs)


def finish_kernel(item, items, surface, pieces, *refs):
    last = item == items - 1
    slice_ref, known_ref, face_ref = refs[:3]
    refs = refs[3:]
    if item == 0:
        own_ref, refs = refs[0], refs[1:]
    else:
        sides, refs = refs[:4], refs[4:]
    earlier_refs, refs = (refs[:item], refs[item:]) if last else ((), refs)
    out_ref, refs = refs[0], refs[1:]
    if item == 0:
        sides, refs = refs[:4], refs[4:]
    side_high_ref, side_low_ref, across_high_ref, across_low_ref = sides
    if item == 0:
        wide_ref = refs[0]
    order_size = known_ref.shape[-1]
    corner = order_size - surface
    slice_now = slice_ref[0]
    if item == 0:
        wide_ref[...] = jnp.zeros_like(wide_ref)

        @pl.when(slice_now == 0)
        def _():
            wide_ref[corner:, :surface] = own_ref[parts, :, :surface]
            plain = wide_ref[...]
            side_high_ref[...], side_low_ref[...] = split_pair(plain[:, :surface])
            across_high_ref[...], across_low_ref[...] = split_pair(plain.T)

        @pl.when(slice_now != 0)
        def _():
            wide_ref[corner:, :surface] = face_ref[parts, :, :surface]
            plain = wide_ref[...]
            side_high_ref[:surface], side_low_ref[:surface] = split_pair(face_ref[parts, :, :surface].T)
            side_high_ref[surface:] = jnp.zeros((corner, surface), jnp.bfloat16)
            side_low_ref[surface:] = jnp.zeros((corner, surface), jnp.bfloat16)
            across_high_ref[...], across_low_ref[...] = split_pair(plain)

    side = (side_high_ref[...], side_low_ref[...])
    across = (across_high_ref[...], across_low_ref[...])
    (through_real,) = product_stacked([side], split_pair(face_ref[0]))
    (through_imag,) = product_stacked([side], split_pair(face_ref[1]))
    term_real, term_imag = product_stacked([split_pair(through_real), split_pair(through_imag)], across)
    green = inverse_pair(known_ref[0] - term_real, known_ref[1] - term_imag)
    for piece, segments in enumerate(pieces):
        filled = 0
        for part, row, count in segments:
            target = (piece, item) if last else (piece,)
            out_ref[target + (slice(filled, filled + count), slice(None))] = green[part][row : row + count, :]
            filled += count
    for place, earlier_ref in enumerate(earlier_refs):
        out_ref[:, place] = earlier_ref[...]


def scatter_kernel(
    energies_all, momenta_all, energies_here, momenta_here, momentum_groups, branches, slots,
    group_ref, factor_ref, pattern_ref, in_ref, out_ref, mixed_ref,
):
    table_size = momenta_all * momenta_all
    offsets = [jnp.max(factor_ref[table_size + branches + branch]).astype(jnp.int32) for branch in range(branches)]

    def place(energy, momentum):
        group = (energy // energies_here) * momentum_groups + momentum // momenta_here
        return slots[group], (energy % energies_here) * momenta_here + momentum % momenta_here

    piece_rows = in_ref.shape[2]
    per_energy = pattern_ref.shape[1]
    if piece_rows <= per_energy:
        first = lax.rem(group_ref[0] * piece_rows, per_energy)
        mask = pattern_ref[0, pl.ds(pl.multiple_of(first, piece_rows), piece_rows), :]
    else:
        mask = jnp.concatenate([pattern_ref[0]] * (piece_rows // per_energy), axis=0)
    mask = mask.astype(jnp.float32)
    mixed_ref[energies_all] = jnp.zeros(mixed_ref.shape[1:], jnp.float32)
    for energy in range(energies_all):
        blocks = [in_ref[place(energy, momentum)] for momentum in range(momenta_all)]
        for target in range(momenta_all):
            total = factor_ref[target * momenta_all] * blocks[0]
            for momentum in range(1, momenta_all):
                total = total + factor_ref[target * momenta_all + momentum] * blocks[momentum]
            mixed_ref[energy, target] = total
    for energy in range(energies_all):
        sources = []
        for branch in range(branches):
            below = energy - offsets[branch]
            above = energy + offsets[branch]
            below = jnp.where(jnp.logical_and(below >= 0, below < energies_all), below, energies_all)
            above = jnp.where(jnp.logical_and(above >= 0, above < energies_all), above, energies_all)
            sources.append((factor_ref[table_size + branch], below, above))
        for target in range(momenta_all):
            total = None
            for strength, below, above in sources:
                term = strength * (mixed_ref[below, target] + mixed_ref[above, target])
                total = term if total is None else total + term
            out_ref[place(energy, target)] = total * mask


def momentum_coefficients(momentum_table, momentum_weights):
    momentum_count = momentum_table.shape[0]
    labels = jnp.arange(momentum_count, dtype=jnp.int32)
    matches = momentum_table[:, :, None] == labels[None, None, :]
    return jnp.sum(jnp.where(matches, momentum_weights[None, :, None], 0.0), axis=1)


def assemble_kernel(pieces, in_ref, out_ref, semaphores):
    copies = []
    for item in range(out_ref.shape[0]):
        for slot, segments in enumerate(pieces):
            filled = 0
            for part, row, count in segments:
                source = in_ref.at[slot, item, pl.ds(filled, count)]
                target = out_ref.at[item, part, pl.ds(row, count)]
                copies.append(pltpu.make_async_copy(source, target, semaphores.at[len(copies)]))
                filled += count
    for copy in copies:
        copy.start()
    for copy in copies:
        copy.wait()


def member_order(count):
    return [int(member) for member in np.random.RandomState(member_seed).permutation(count)]


def row_pieces(order_size, energy_groups, momentum_groups):
    per_energy = order_size // energy_groups
    piece_rows = parts * per_energy // momentum_groups
    pieces = []
    for energy_group in range(energy_groups):
        for momentum_group in range(momentum_groups):
            start, left, segments = momentum_group * piece_rows, piece_rows, []
            while left:
                part, inside = divmod(start, per_energy)
                count = min(left, per_energy - inside)
                segments.append((part, energy_group * per_energy + inside, count))
                start, left = start + count, left - count
            pieces.append(segments)
    return piece_rows, pieces


def product_split(left_side, right_side):
    return product(split_pair(left_side), split_pair(right_side))


def green_by_sweeps(hamiltonian, coupling, self_blocks, shift, position, slices):
    orbitals, surface = hamiltonian.shape[-1], coupling.shape[-1]
    corner = orbitals - surface
    identity = jnp.eye(orbitals, dtype=jnp.float32)
    symmetric = 0.5 * (hamiltonian + hamiltonian.T)
    system = jnp.stack(
        [
            shift[:, None, None] * identity - symmetric - self_blocks[:, 0],
            broadening * identity - self_blocks[:, 1],
        ],
        axis=1,
    )
    source = jnp.stack([jnp.zeros((surface, surface)), -contact * jnp.eye(surface)]).astype(jnp.float32)
    source = jnp.broadcast_to(source, (system.shape[0],) + source.shape)
    over_parts = jax.vmap(jax.vmap(product_split, (None, 0)), (None, 0))
    over_parts_right = jax.vmap(jax.vmap(product_split, (0, None)), (0, None))
    around = ((0, 0), (0, 0))

    def less_first(matrix, term):
        return matrix - jnp.pad(term, around + ((0, corner), (0, corner)))

    def less_last(matrix, term):
        return matrix - jnp.pad(term, around + ((corner, 0), (corner, 0)))

    def inverse(matrix):
        return jnp.stack(jax.vmap(inverse_pair)(matrix[:, 0], matrix[:, 1]), axis=1)

    def through(side, middle):
        return over_parts_right(over_parts(side, middle), side.T)

    left = source
    right = through(coupling, source)
    for turn in range(slices - 1):
        face = inverse(less_first(system, left))[..., corner:, corner:]
        moved = lax.ppermute(through(coupling.T, face), "space", [(i, i + 1) for i in range(slices - 1)])
        left = jnp.where(position == turn + 1, moved, left)
        face = inverse(less_last(system, right))[..., :surface, :surface]
        moved = lax.ppermute(face, "space", [(i + 1, i) for i in range(slices - 1)])
        right = jnp.where(position == slices - 2 - turn, through(coupling, moved), right)
    return inverse(less_last(less_first(system, left), right))


def cut_pieces(green, pieces):
    return jnp.stack(
        [
            jnp.concatenate([green[:, part, row : row + count] for part, row, count in segments], axis=1)
            for segments in pieces
        ]
    )


def on_chip(*block):
    return pl.BlockSpec(memory_space=pltpu.SMEM)


float_vmem = functools.partial(pltpu.VMEM, dtype=jnp.float32)


def green_two_slices(hamiltonian, coupling, self_blocks, shift, position, pieces, blocks_shape, small):
    orbitals, surface = hamiltonian.shape[-1], coupling.shape[-1]
    items = self_blocks.shape[0]
    slice_now = position.astype(jnp.int32).reshape(1)
    order = (orbitals, orbitals)
    pair = (parts,) + order
    floats = functools.partial(jax.ShapeDtypeStruct, dtype=jnp.float32)
    halves = functools.partial(jax.ShapeDtypeStruct, dtype=jnp.bfloat16)
    whole = pl.BlockSpec(memory_space=pltpu.VMEM)
    far = pl.BlockSpec(memory_space=pltpu.HBM)
    params = pltpu.CompilerParams(vmem_limit_bytes=kernel_memory)
    inverse_flops = 18 * orbitals**3
    swap = [(0, 1), (1, 0)]

    shift = jnp.broadcast_to(shift[:, None, None], (items, 1, orbitals))
    self_blocks, base, term = (
        pltpu.with_memory_space_constraint(array, pltpu.HBM) for array in (self_blocks, hamiltonian, coupling)
    )
    small = [pltpu.with_memory_space_constraint(array, pltpu.HBM) for array in small]
    factor_count = small[0].size + small[2].size + small[3].size
    known, faces, sent = [], [], []
    later = []
    for item in range(items):
        first = item == 0
        scratch = []
        if first:
            scratch += [float_vmem(pair), float_vmem(order), float_vmem((surface, surface)), float_vmem(order)]
            scratch += [pltpu.SMEM(array.shape, array.dtype) for array in small]
            scratch += [pltpu.SemaphoreType.DMA((2 + items * parts,)), pltpu.SemaphoreType.DMA((len(small),))]
        extra_shapes = []
        if first:
            extra_shapes = [floats(order), floats(order), floats((factor_count, 1, orbitals))]
            extra_shapes += [floats(pair)] * (items - 1)
        result = pl.pallas_call(
            functools.partial(start_kernel, item, items, surface),
            in_specs=[on_chip(), whole] + ([far] * (3 + len(small)) if first else [whole] * 3),
            out_specs=[whole] * (2 + len(extra_shapes)),
            out_shape=[floats(pair), floats((parts + first, surface, orbitals))] + extra_shapes,
            scratch_shapes=scratch,
            compiler_params=params,
            cost_estimate=pl.CostEstimate(flops=inverse_flops, bytes_accessed=0, transcendentals=0),
            name=f"start{item}",
        )(slice_now, shift, base, term, *([self_blocks] + small if first else [later[item - 1]]))
        known.append(result[0])
        if first:
            base, term, factors, *later = result[2:]
        sent.append(result[1])
        faces.append(lax.ppermute(result[1], "space", swap))

    greens, sides = [], []
    for item in range(items):
        first, last = item == 0, item == items - 1
        operands = [slice_now, known[item], faces[item]] + ([sent[item]] if first else sides) + (greens if last else [])
        out_shape = [floats(blocks_shape if last else blocks_shape[:1] + blocks_shape[2:])]
        result = pl.pallas_call(
            functools.partial(finish_kernel, item, items, surface, pieces),
            in_specs=[on_chip()] + [whole] * (len(operands) - 1),
            out_specs=[whole] * (5 if first else 1),
            out_shape=out_shape + ([halves((orbitals, surface))] * 2 + [halves(order)] * 2 if first else []),
            scratch_shapes=[float_vmem(order)] if first else [],
            compiler_params=params,
            cost_estimate=pl.CostEstimate(flops=2 * inverse_flops, bytes_accessed=0, transcendentals=0),
            name=f"finish{item}",
        )(*operands)
        greens.append(result[0])
        if first:
            sides = list(result[1:])
    return greens[-1], factors


def body(
    hamiltonian,
    coupling,
    self_energy,
    pattern,
    momentum_table,
    momentum_weights,
    mode_strengths,
    mode_offsets,
):
    orbitals = hamiltonian.shape[-1]
    surface = coupling.shape[-1]
    energies_here = self_energy.shape[1]
    momenta_here = self_energy.shape[2]
    energy_groups = lax.axis_size("energy")
    momentum_groups = lax.axis_size("mom")
    position = lax.axis_index("space")
    energies_all = energies_here * energy_groups
    momenta_all = momenta_here * momentum_groups
    items = energies_here * momenta_here
    branches = mode_offsets.shape[0]
    energy_index = lax.axis_index("energy") * energies_here + jnp.arange(energies_here, dtype=jnp.int32)
    momentum_index = lax.axis_index("mom") * momenta_here + jnp.arange(momenta_here, dtype=jnp.int32)
    energy = -2.0 + 4.0 * energy_index.astype(jnp.float32) / energies_all
    angle = 2.0 * jnp.pi * momentum_index.astype(jnp.float32) / momenta_all
    kinetic = dispersion * (1.0 - jnp.cos(angle))
    shift = (energy[:, None] - kinetic[None, :]).reshape(items)
    self_blocks = self_energy.reshape(items, parts, orbitals, orbitals)
    piece_rows, pieces = row_pieces(orbitals, energy_groups, momentum_groups)
    members = member_order(len(pieces))
    slots = [members.index(group) for group in range(len(members))]
    pieces = [pieces[member] for member in members]
    blocks_shape = (len(pieces), items, piece_rows, orbitals)
    if lax.axis_size("space") == 2:
        small = (momentum_table, momentum_weights, mode_strengths, mode_offsets)
        green, factors = green_two_slices(
            hamiltonian, coupling, self_blocks, shift, position, pieces, blocks_shape, small
        )
    else:
        slices = lax.axis_size("space")
        green = green_by_sweeps(hamiltonian[0], coupling[0], self_blocks, shift, position, slices)
        green = cut_pieces(green, pieces)
        factors = momentum_coefficients(momentum_table, momentum_weights).reshape(-1)
        factors = jnp.concatenate([factors, mode_strengths, mode_offsets.astype(jnp.float32)])
        factors = jnp.broadcast_to(factors[:, None, None], (factors.shape[0], 1, orbitals))

    exchange = functools.partial(
        lax.all_to_all,
        axis_name=("energy", "mom"),
        split_axis=0,
        concat_axis=0,
        axis_index_groups=[members],
        tiled=True,
    )
    momentum_group = lax.axis_index("mom").astype(jnp.int32).reshape(1)
    gathered = exchange(green)
    scattered = pl.pallas_call(
        functools.partial(
            scatter_kernel, energies_all, momenta_all, energies_here, momenta_here, momentum_groups, branches, slots
        ),
        in_specs=[on_chip()] + [pl.BlockSpec(memory_space=pltpu.VMEM)] * 3,
        out_shape=jax.ShapeDtypeStruct(blocks_shape, jnp.float32),
        scratch_shapes=[float_vmem((energies_all + 1, momenta_all, piece_rows, orbitals))],
        compiler_params=pltpu.CompilerParams(vmem_limit_bytes=kernel_memory),
        name="scatter",
    )(momentum_group, factors, pattern, gathered)
    returned = exchange(scattered)
    copies = items * sum(len(segments) for segments in pieces)
    whole = pl.pallas_call(
        functools.partial(assemble_kernel, pieces),
        in_specs=[pl.BlockSpec(memory_space=pltpu.VMEM)],
        out_specs=pl.BlockSpec(memory_space=pltpu.HBM),
        out_shape=jax.ShapeDtypeStruct((items, parts, orbitals, orbitals), jnp.float32),
        scratch_shapes=[pltpu.SemaphoreType.DMA((copies,))],
        compiler_params=pltpu.CompilerParams(vmem_limit_bytes=kernel_memory),
        name="assemble",
    )(returned)
    return whole.reshape(1, energies_here, momenta_here, parts, orbitals, orbitals)


def solution(mesh):
    return jax.shard_map(
        body,
        mesh=mesh,
        in_specs=(
            P("space", None, None),
            P("space", None, None),
            P("space", "energy", "mom", None, None, None),
            P("space", "energy", None),
            P(),
            P(),
            P(),
            P(),
        ),
        out_specs=P("space", "energy", "mom", None, None, None),
        check_vma=False,
    )
```

```python
import functools

import jax
import jax.numpy as jnp
import numpy as np
from jax import lax
from jax.experimental import pallas as pl
from jax.experimental.pallas import tpu as pltpu
from jax.sharding import PartitionSpec as P

broadening = 1.0
contact = 1.0
dispersion = 1.0
parts = 2
kernel_memory = 24 * 1024 * 1024
member_seed = 79


def split_pair(value):
    high = value.astype(jnp.bfloat16)
    return high, (value - high.astype(jnp.float32)).astype(jnp.bfloat16)


def product(left_pair, right_pair):
    left_high, left_low = left_pair
    right_high, right_low = right_pair
    dot = functools.partial(jnp.dot, preferred_element_type=jnp.float32)
    return dot(left_high, right_high) + dot(left_high, right_low) + dot(left_low, right_high)


def diagonal_mask(order_size):
    rows = lax.broadcasted_iota(jnp.int32, (order_size, order_size), 0)
    columns = lax.broadcasted_iota(jnp.int32, (order_size, order_size), 1)
    return rows == columns


def product_stacked(left_pairs, right_pair):
    rows = left_pairs[0][0].shape[0]
    count = len(left_pairs)
    right_high, right_low = right_pair
    highs = [pair[0] for pair in left_pairs]
    lows = [pair[1] for pair in left_pairs]
    dot = functools.partial(jnp.dot, preferred_element_type=jnp.float32)
    with_high = dot(jnp.concatenate(highs + lows, axis=0), right_high)
    with_low = dot(jnp.concatenate(highs, axis=0), right_low)
    return [
        with_high[i * rows : (i + 1) * rows]
        + with_high[(count + i) * rows : (count + i + 1) * rows]
        + with_low[i * rows : (i + 1) * rows]
        for i in range(count)
    ]


def inverse_pair(real_part, imag_part):
    order_size = real_part.shape[-1]
    on_diagonal = diagonal_mask(order_size)
    diag_real = jnp.sum(jnp.where(on_diagonal, real_part, 0.0), axis=0, keepdims=True)
    diag_imag = jnp.sum(jnp.where(on_diagonal, imag_part, 0.0), axis=0, keepdims=True)
    modulus = diag_real * diag_real + diag_imag * diag_imag
    column_real = diag_real / modulus
    column_imag = -diag_imag / modulus
    row_real = jnp.sum(jnp.where(on_diagonal, column_real, 0.0), axis=1, keepdims=True)
    row_imag = jnp.sum(jnp.where(on_diagonal, column_imag, 0.0), axis=1, keepdims=True)
    off_real = jnp.where(on_diagonal, 0.0, real_part)
    off_imag = jnp.where(on_diagonal, 0.0, imag_part)
    scaled_real = row_real * off_real - row_imag * off_imag
    scaled_imag = row_real * off_imag + row_imag * off_real
    pair_real = split_pair(scaled_real)
    pair_imag = split_pair(scaled_imag)
    pair_both = split_pair(scaled_real + scaled_imag)
    (square_real,) = product_stacked([pair_real], pair_real)
    (square_imag,) = product_stacked([pair_imag], pair_imag)
    (square_both,) = product_stacked([pair_both], pair_both)
    series_real = square_real - square_imag - scaled_real + jnp.where(on_diagonal, 1.0, 0.0)
    series_imag = square_both - square_real - square_imag - scaled_imag
    return (
        series_real * column_real - series_imag * column_imag,
        series_real * column_imag + series_imag * column_real,
    )


def write_factors(factor_ref, table_ref, weight_ref, strength_ref, offset_ref):
    momenta_all, branches = weight_ref.shape[0], strength_ref.shape[0]
    values = []
    for target in range(momenta_all):
        for source in range(momenta_all):
            total = jnp.float32(0.0)
            for transfer in range(momenta_all):
                total += jnp.where(table_ref[target, transfer] == source, weight_ref[transfer], 0.0)
            values.append(total)
    values += [strength_ref[branch] for branch in range(branches)]
    values += [offset_ref[branch].astype(jnp.float32) for branch in range(branches)]
    for place, value in enumerate(values):
        factor_ref[place] = jnp.full(factor_ref.shape[1:], value, jnp.float32)


def start_kernel(item, items, surface, slice_ref, shift_ref, base_from_ref, term_from_ref, *rest):
    slice_now = slice_ref[0]
    if item == 0:
        self_from_ref, small_refs = rest[0], rest[1:5]
        known_ref, face_ref, base_ref, term_ref, factor_ref = rest[5:10]
        later_refs = rest[10 : 9 + items]
        self_ref, base_buffer, coupling_buffer, wide_ref = rest[9 + items : 13 + items]
        near_refs, semaphores, small_semaphores = rest[13 + items : 17 + items], rest[-2], rest[-1]
        small_copies = [
            pltpu.make_async_copy(small_ref, near_ref, small_semaphores.at[place])
            for place, (small_ref, near_ref) in enumerate(zip(small_refs, near_refs))
        ]
        self_copies = []
        for place, target_ref in enumerate((self_ref,) + later_refs):
            for part in range(parts):
                semaphore = semaphores.at[2 + place * parts + part]
                copy = pltpu.make_async_copy(self_from_ref.at[place, part], target_ref.at[part], semaphore)
                self_copies.append(copy)
        coupling_copy = pltpu.make_async_copy(term_from_ref.at[0], coupling_buffer, semaphores.at[0])
        base_copy = pltpu.make_async_copy(base_from_ref.at[0], base_buffer, semaphores.at[1])
        for copy in small_copies + [coupling_copy, base_copy] + self_copies:
            copy.start()
    else:
        self_ref, known_ref, face_ref = rest
        base_ref, term_ref = base_from_ref, term_from_ref
    order_size = known_ref.shape[-1]
    corner = order_size - surface
    on_diagonal = diagonal_mask(order_size)
    if item == 0:
        coupling_copy.wait()
        face_ref[parts] = jnp.zeros(face_ref.shape[1:], jnp.float32)
        face_ref[parts, :, :surface] = coupling_buffer[...]

        @pl.when(slice_now == 0)
        def _():
            rows = lax.broadcasted_iota(jnp.int32, (order_size, order_size), 0)
            inside = jnp.logical_and(on_diagonal, rows < surface)
            term_ref[...] = jnp.where(inside, contact, 0.0)

        @pl.when(slice_now != 0)
        def _():
            wide_ref[...] = jnp.zeros_like(wide_ref)
            wide_ref[corner:, :surface] = coupling_buffer[...]
            wide = wide_ref[...]
            term_ref[...] = contact * product(split_pair(wide), split_pair(wide.T))

        base_copy.wait()
        base_ref[...] = 0.5 * (base_buffer[...] + base_buffer[...].T)
        for copy in small_copies:
            copy.wait()
        write_factors(factor_ref, *near_refs)
        for copy in self_copies[:parts]:
            copy.wait()
    real_part = jnp.where(on_diagonal, shift_ref[item], 0.0) - base_ref[...] - self_ref[0]
    imag_part = jnp.where(on_diagonal, broadening, 0.0) - self_ref[1] + term_ref[...]
    known_ref[0] = real_part
    known_ref[1] = imag_part
    green_real, green_imag = inverse_pair(real_part, imag_part)

    @pl.when(slice_now == 0)
    def _():
        face_ref[0] = green_real[corner:]
        face_ref[1] = green_imag[corner:]

    @pl.when(slice_now != 0)
    def _():
        face_ref[0] = green_real[:surface]
        face_ref[1] = green_imag[:surface]

    if item == 0:
        for copy in self_copies[parts:]:
            copy.wait()


def finish_kernel(item, items, surface, pieces, *refs):
    last = item == items - 1
    slice_ref, known_ref, face_ref = refs[:3]
    refs = refs[3:]
    if item == 0:
        own_ref, refs = refs[0], refs[1:]
    else:
        sides, refs = refs[:4], refs[4:]
    earlier_refs, refs = (refs[:item], refs[item:]) if last else ((), refs)
    out_ref, refs = refs[0], refs[1:]
    if item == 0:
        sides, refs = refs[:4], refs[4:]
    side_high_ref, side_low_ref, across_high_ref, across_low_ref = sides
    if item == 0:
        wide_ref = refs[0]
    order_size = known_ref.shape[-1]
    corner = order_size - surface
    slice_now = slice_ref[0]
    if item == 0:
        wide_ref[...] = jnp.zeros_like(wide_ref)

        @pl.when(slice_now == 0)
        def _():
            wide_ref[corner:, :surface] = own_ref[parts, :, :surface]
            plain = wide_ref[...]
            side_high_ref[...], side_low_ref[...] = split_pair(plain[:, :surface])
            across_high_ref[...], across_low_ref[...] = split_pair(plain.T)

        @pl.when(slice_now != 0)
        def _():
            wide_ref[corner:, :surface] = face_ref[parts, :, :surface]
            plain = wide_ref[...]
            side_high_ref[:surface], side_low_ref[:surface] = split_pair(face_ref[parts, :, :surface].T)
            side_high_ref[surface:] = jnp.zeros((corner, surface), jnp.bfloat16)
            side_low_ref[surface:] = jnp.zeros((corner, surface), jnp.bfloat16)
            across_high_ref[...], across_low_ref[...] = split_pair(plain)

    side = (side_high_ref[...], side_low_ref[...])
    across = (across_high_ref[...], across_low_ref[...])
    (through_real,) = product_stacked([side], split_pair(face_ref[0]))
    (through_imag,) = product_stacked([side], split_pair(face_ref[1]))
    term_real, term_imag = product_stacked([split_pair(through_real), split_pair(through_imag)], across)
    green = inverse_pair(known_ref[0] - term_real, known_ref[1] - term_imag)
    for piece, segments in enumerate(pieces):
        filled = 0
        for part, row, count in segments:
            target = (piece, item) if last else (piece,)
            out_ref[target + (slice(filled, filled + count), slice(None))] = green[part][row : row + count, :]
            filled += count
    for place, earlier_ref in enumerate(earlier_refs):
        out_ref[:, place] = earlier_ref[...]


def scatter_kernel(
    energies_all, momenta_all, energies_here, momenta_here, momentum_groups, branches, slots,
    group_ref, factor_ref, pattern_ref, in_ref, out_ref, mixed_ref,
):
    table_size = momenta_all * momenta_all
    offsets = [jnp.max(factor_ref[table_size + branches + branch]).astype(jnp.int32) for branch in range(branches)]

    def place(energy, momentum):
        group = (energy // energies_here) * momentum_groups + momentum // momenta_here
        return slots[group], (energy % energies_here) * momenta_here + momentum % momenta_here

    piece_rows = in_ref.shape[2]
    per_energy = pattern_ref.shape[1]
    if piece_rows <= per_energy:
        first = lax.rem(group_ref[0] * piece_rows, per_energy)
        mask = pattern_ref[0, pl.ds(pl.multiple_of(first, piece_rows), piece_rows), :]
    else:
        mask = jnp.concatenate([pattern_ref[0]] * (piece_rows // per_energy), axis=0)
    mask = mask.astype(jnp.float32)
    mixed_ref[energies_all] = jnp.zeros(mixed_ref.shape[1:], jnp.float32)
    for energy in range(energies_all):
        blocks = [in_ref[place(energy, momentum)] for momentum in range(momenta_all)]
        for target in range(momenta_all):
            total = factor_ref[target * momenta_all] * blocks[0]
            for momentum in range(1, momenta_all):
                total = total + factor_ref[target * momenta_all + momentum] * blocks[momentum]
            mixed_ref[energy, target] = total
    for energy in range(energies_all):
        sources = []
        for branch in range(branches):
            below = energy - offsets[branch]
            above = energy + offsets[branch]
            below = jnp.where(jnp.logical_and(below >= 0, below < energies_all), below, energies_all)
            above = jnp.where(jnp.logical_and(above >= 0, above < energies_all), above, energies_all)
            sources.append((factor_ref[table_size + branch], below, above))
        for target in range(momenta_all):
            total = None
            for strength, below, above in sources:
                term = strength * (mixed_ref[below, target] + mixed_ref[above, target])
                total = term if total is None else total + term
            out_ref[place(energy, target)] = total * mask


def momentum_coefficients(momentum_table, momentum_weights):
    momentum_count = momentum_table.shape[0]
    labels = jnp.arange(momentum_count, dtype=jnp.int32)
    matches = momentum_table[:, :, None] == labels[None, None, :]
    return jnp.sum(jnp.where(matches, momentum_weights[None, :, None], 0.0), axis=1)


def assemble_kernel(pieces, in_ref, out_ref, semaphores):
    copies = []
    for item in range(out_ref.shape[0]):
        for slot, segments in enumerate(pieces):
            filled = 0
            for part, row, count in segments:
                source = in_ref.at[slot, item, pl.ds(filled, count)]
                target = out_ref.at[item, part, pl.ds(row, count)]
                copies.append(pltpu.make_async_copy(source, target, semaphores.at[len(copies)]))
                filled += count
    for copy in copies:
        copy.start()
    for copy in copies:
        copy.wait()


def member_order(count):
    return [int(member) for member in np.random.RandomState(member_seed).permutation(count)]


def row_pieces(order_size, energy_groups, momentum_groups):
    per_energy = order_size // energy_groups
    piece_rows = parts * per_energy // momentum_groups
    pieces = []
    for energy_group in range(energy_groups):
        for momentum_group in range(momentum_groups):
            start, left, segments = momentum_group * piece_rows, piece_rows, []
            while left:
                part, inside = divmod(start, per_energy)
                count = min(left, per_energy - inside)
                segments.append((part, energy_group * per_energy + inside, count))
                start, left = start + count, left - count
            pieces.append(segments)
    return piece_rows, pieces


def product_split(left_side, right_side):
    return product(split_pair(left_side), split_pair(right_side))


def green_by_sweeps(hamiltonian, coupling, self_blocks, shift, position, slices):
    orbitals, surface = hamiltonian.shape[-1], coupling.shape[-1]
    corner = orbitals - surface
    identity = jnp.eye(orbitals, dtype=jnp.float32)
    symmetric = 0.5 * (hamiltonian + hamiltonian.T)
    system = jnp.stack(
        [
            shift[:, None, None] * identity - symmetric - self_blocks[:, 0],
            broadening * identity - self_blocks[:, 1],
        ],
        axis=1,
    )
    source = jnp.stack([jnp.zeros((surface, surface)), -contact * jnp.eye(surface)]).astype(jnp.float32)
    source = jnp.broadcast_to(source, (system.shape[0],) + source.shape)
    over_parts = jax.vmap(jax.vmap(product_split, (None, 0)), (None, 0))
    over_parts_right = jax.vmap(jax.vmap(product_split, (0, None)), (0, None))
    around = ((0, 0), (0, 0))

    def less_first(matrix, term):
        return matrix - jnp.pad(term, around + ((0, corner), (0, corner)))

    def less_last(matrix, term):
        return matrix - jnp.pad(term, around + ((corner, 0), (corner, 0)))

    def inverse(matrix):
        return jnp.stack(jax.vmap(inverse_pair)(matrix[:, 0], matrix[:, 1]), axis=1)

    def through(side, middle):
        return over_parts_right(over_parts(side, middle), side.T)

    left = source
    right = through(coupling, source)
    for turn in range(slices - 1):
        face = inverse(less_first(system, left))[..., corner:, corner:]
        moved = lax.ppermute(through(coupling.T, face), "space", [(i, i + 1) for i in range(slices - 1)])
        left = jnp.where(position == turn + 1, moved, left)
        face = inverse(less_last(system, right))[..., :surface, :surface]
        moved = lax.ppermute(face, "space", [(i + 1, i) for i in range(slices - 1)])
        right = jnp.where(position == slices - 2 - turn, through(coupling, moved), right)
    return inverse(less_last(less_first(system, left), right))


def cut_pieces(green, pieces):
    return jnp.stack(
        [
            jnp.concatenate([green[:, part, row : row + count] for part, row, count in segments], axis=1)
            for segments in pieces
        ]
    )


def on_chip(*block):
    return pl.BlockSpec(memory_space=pltpu.SMEM)


float_vmem = functools.partial(pltpu.VMEM, dtype=jnp.float32)


def green_two_slices(hamiltonian, coupling, self_blocks, shift, position, pieces, blocks_shape, small):
    orbitals, surface = hamiltonian.shape[-1], coupling.shape[-1]
    items = self_blocks.shape[0]
    slice_now = position.astype(jnp.int32).reshape(1)
    order = (orbitals, orbitals)
    pair = (parts,) + order
    floats = functools.partial(jax.ShapeDtypeStruct, dtype=jnp.float32)
    halves = functools.partial(jax.ShapeDtypeStruct, dtype=jnp.bfloat16)
    whole = pl.BlockSpec(memory_space=pltpu.VMEM)
    far = pl.BlockSpec(memory_space=pltpu.HBM)
    params = pltpu.CompilerParams(vmem_limit_bytes=kernel_memory)
    inverse_flops = 18 * orbitals**3
    swap = [(0, 1), (1, 0)]

    shift = jnp.broadcast_to(shift[:, None, None], (items, 1, orbitals))
    self_blocks, base, term = (
        pltpu.with_memory_space_constraint(array, pltpu.HBM) for array in (self_blocks, hamiltonian, coupling)
    )
    small = [pltpu.with_memory_space_constraint(array, pltpu.HBM) for array in small]
    factor_count = small[0].size + small[2].size + small[3].size
    known, faces, sent = [], [], []
    later = []
    for item in range(items):
        first = item == 0
        scratch = []
        if first:
            scratch += [float_vmem(pair), float_vmem(order), float_vmem((surface, surface)), float_vmem(order)]
            scratch += [pltpu.SMEM(array.shape, array.dtype) for array in small]
            scratch += [pltpu.SemaphoreType.DMA((2 + items * parts,)), pltpu.SemaphoreType.DMA((len(small),))]
        extra_shapes = []
        if first:
            extra_shapes = [floats(order), floats(order), floats((factor_count, 1, orbitals))]
            extra_shapes += [floats(pair)] * (items - 1)
        result = pl.pallas_call(
            functools.partial(start_kernel, item, items, surface),
            in_specs=[on_chip(), whole] + ([far] * (3 + len(small)) if first else [whole] * 3),
            out_specs=[whole] * (2 + len(extra_shapes)),
            out_shape=[floats(pair), floats((parts + first, surface, orbitals))] + extra_shapes,
            scratch_shapes=scratch,
            compiler_params=params,
            cost_estimate=pl.CostEstimate(flops=inverse_flops, bytes_accessed=0, transcendentals=0),
            name=f"start{item}",
        )(slice_now, shift, base, term, *([self_blocks] + small if first else [later[item - 1]]))
        known.append(result[0])
        if first:
            base, term, factors, *later = result[2:]
        sent.append(result[1])
        faces.append(lax.ppermute(result[1], "space", swap))

    greens, sides = [], []
    for item in range(items):
        first, last = item == 0, item == items - 1
        operands = [slice_now, known[item], faces[item]] + ([sent[item]] if first else sides) + (greens if last else [])
        out_shape = [floats(blocks_shape if last else blocks_shape[:1] + blocks_shape[2:])]
        result = pl.pallas_call(
            functools.partial(finish_kernel, item, items, surface, pieces),
            in_specs=[on_chip()] + [whole] * (len(operands) - 1),
            out_specs=[whole] * (5 if first else 1),
            out_shape=out_shape + ([halves((orbitals, surface))] * 2 + [halves(order)] * 2 if first else []),
            scratch_shapes=[float_vmem(order)] if first else [],
            compiler_params=params,
            cost_estimate=pl.CostEstimate(flops=2 * inverse_flops, bytes_accessed=0, transcendentals=0),
            name=f"finish{item}",
        )(*operands)
        greens.append(result[0])
        if first:
            sides = list(result[1:])
    return greens[-1], factors


def body(
    hamiltonian,
    coupling,
    self_energy,
    pattern,
    momentum_table,
    momentum_weights,
    mode_strengths,
    mode_offsets,
):
    orbitals = hamiltonian.shape[-1]
    surface = coupling.shape[-1]
    energies_here = self_energy.shape[1]
    momenta_here = self_energy.shape[2]
    energy_groups = lax.axis_size("energy")
    momentum_groups = lax.axis_size("mom")
    position = lax.axis_index("space")
    energies_all = energies_here * energy_groups
    momenta_all = momenta_here * momentum_groups
    items = energies_here * momenta_here
    branches = mode_offsets.shape[0]
    energy_index = lax.axis_index("energy") * energies_here + jnp.arange(energies_here, dtype=jnp.int32)
    momentum_index = lax.axis_index("mom") * momenta_here + jnp.arange(momenta_here, dtype=jnp.int32)
    energy = -2.0 + 4.0 * energy_index.astype(jnp.float32) / energies_all
    angle = 2.0 * jnp.pi * momentum_index.astype(jnp.float32) / momenta_all
    kinetic = dispersion * (1.0 - jnp.cos(angle))
    shift = (energy[:, None] - kinetic[None, :]).reshape(items)
    self_blocks = self_energy.reshape(items, parts, orbitals, orbitals)
    piece_rows, pieces = row_pieces(orbitals, energy_groups, momentum_groups)
    members = member_order(len(pieces))
    slots = [members.index(group) for group in range(len(members))]
    pieces = [pieces[member] for member in members]
    blocks_shape = (len(pieces), items, piece_rows, orbitals)
    if lax.axis_size("space") == 2:
        small = (momentum_table, momentum_weights, mode_strengths, mode_offsets)
        green, factors = green_two_slices(
            hamiltonian, coupling, self_blocks, shift, position, pieces, blocks_shape, small
        )
    else:
        slices = lax.axis_size("space")
        green = green_by_sweeps(hamiltonian[0], coupling[0], self_blocks, shift, position, slices)
        green = cut_pieces(green, pieces)
        factors = momentum_coefficients(momentum_table, momentum_weights).reshape(-1)
        factors = jnp.concatenate([factors, mode_strengths, mode_offsets.astype(jnp.float32)])
        factors = jnp.broadcast_to(factors[:, None, None], (factors.shape[0], 1, orbitals))

    exchange = functools.partial(
        lax.all_to_all,
        axis_name=("energy", "mom"),
        split_axis=0,
        concat_axis=0,
        axis_index_groups=[members],
        tiled=True,
    )
    momentum_group = lax.axis_index("mom").astype(jnp.int32).reshape(1)
    gathered = exchange(green)
    scattered = pl.pallas_call(
        functools.partial(
            scatter_kernel, energies_all, momenta_all, energies_here, momenta_here, momentum_groups, branches, slots
        ),
        in_specs=[on_chip()] + [pl.BlockSpec(memory_space=pltpu.VMEM)] * 3,
        out_shape=jax.ShapeDtypeStruct(blocks_shape, jnp.float32),
        scratch_shapes=[float_vmem((energies_all + 1, momenta_all, piece_rows, orbitals))],
        compiler_params=pltpu.CompilerParams(vmem_limit_bytes=kernel_memory),
        name="scatter",
    )(momentum_group, factors, pattern, gathered)
    returned = exchange(scattered)
    copies = items * sum(len(segments) for segments in pieces)
    whole = pl.pallas_call(
        functools.partial(assemble_kernel, pieces),
        in_specs=[pl.BlockSpec(memory_space=pltpu.VMEM)],
        out_specs=pl.BlockSpec(memory_space=pltpu.HBM),
        out_shape=jax.ShapeDtypeStruct((items, parts, orbitals, orbitals), jnp.float32),
        scratch_shapes=[pltpu.SemaphoreType.DMA((copies,))],
        compiler_params=pltpu.CompilerParams(vmem_limit_bytes=kernel_memory),
        name="assemble",
    )(returned)
    return whole.reshape(1, energies_here, momenta_here, parts, orbitals, orbitals)


def solution(mesh):
    return jax.shard_map(
        body,
        mesh=mesh,
        in_specs=(
            P("space", None, None),
            P("space", None, None),
            P("space", "energy", "mom", None, None, None),
            P("space", "energy", None),
            P(),
            P(),
            P(),
            P(),
        ),
        out_specs=P("space", "energy", "mom", None, None, None),
        check_vma=False,
    )
```
